512 devices in a mesh: depth: 16 (over x, z_hi), plane: 32 (over z_lo, y, core).
Axes of the slice: x: 4, y: 8, z: 8 (z_hi: 4, z_lo: 2; z = z_hi * 2 + z_lo), core: 2. Of those that a mesh axis runs over, the one named last changes fastest.
Arguments:
- volume: bfloat16 [64, 128, 128], P('depth', 'plane'), may hold values from -6 to 6
- cotangent: float32 [64, 128, 128], P('depth', 'plane'), may hold values from -6 to 6
- kernel_in: bfloat16 [27, 32], replicated, may hold values from -1.25 to 1.25
- kernel_mid: bfloat16 [27, 32, 32], replicated, may hold values from -0.21875 to 0.21875
- kernel_out: bfloat16 [27, 32], replicated, may hold values from -0.21875 to 0.21875
- measured: float32 [64, 32, 1024], P('depth'), may hold values from -24 to 24
- angle_ids: int32 [8], replicated, may hold values from 0 to 31, as said below
- ray_bins: int32 [8, 128, 128], P(None, 'plane'), may hold values from 0 to 1023, as said below
Outputs:
- grad_volume: float32 [64, 128, 128], P('depth', 'plane')
- grad_kernel_in: float32 [27, 32], replicated
- grad_kernel_mid: float32 [27, 32, 32], replicated
- grad_kernel_out: float32 [27, 32], replicated
The draws below stay inside these ranges and needn't reach their ends.
Inputs may be any that keep to these rules, and one draw needn't show every extreme that they name: `angle_ids`: each entry names a measured view; the entries are distinct. `ray_bins`: for each view a, the bins follow parallel-beam geometry: a cell's bin is the detector position of its centre projected along the direction of view angle_ids[a], clipped at the detector's ends.
All inputs are finite; a program needn't handle non-finite values.
Results may differ from the reference program's by a relative error of at most 0.0051.
Values may be sent and summed in bfloat16 or wider, within the bound.
No kernel may reach another device: no remote copies, remote signals or barrier semaphores. Data moves between devices by JAX's collectives and lax.ppermute only.
A program may use at most 64 MiB of HBM per device.

```python
import jax
import jax.numpy as jnp
from jax import lax

C = 32
BINS = 1024
ANG = 8
ANG_ALL = 32
W = 128
NZ = 64
NH = 128


def view_table(key):
    order = jax.random.permutation(jax.random.fold_in(key, 11), ANG_ALL)
    return order[:ANG].astype(jnp.int32)


def draw_angle_ids(key, part):
    return view_table(key)


def draw_ray_bins(key, part):
    views = view_table(key)
    tangent = 2 * views - ANG_ALL
    cosine_num = ANG_ALL * ANG_ALL - tangent * tangent
    sine_num = 2 * tangent * ANG_ALL
    denom = ANG_ALL * ANG_ALL + tangent * tangent
    rows_twice = 2 * jnp.arange(NH, dtype=jnp.int32) - (NH - 1)
    cells_twice = 2 * jnp.arange(W, dtype=jnp.int32) - (W - 1)
    stretch = BINS // min(W, NH) + 1
    along = cells_twice[None, None, :] * cosine_num[:, None, None] + rows_twice[None, :, None] * sine_num[:, None, None]
    placed = BINS // 2 + along * stretch // (2 * denom[:, None, None])
    return jnp.clip(placed, 0, BINS - 1).astype(jnp.int32)


def block_levels(own_key, dims, cuts, low, largest):
    level = 1.0
    for axis_at, shards_of in cuts:
        heights = jax.random.uniform(jax.random.fold_in(jax.random.fold_in(own_key, 6), axis_at), (shards_of,), jnp.float32, low / len(cuts), largest / len(cuts))
        level = level * jnp.repeat(jnp.exp(heights), dims[axis_at] // shards_of).reshape((-1,) + (1,) * (len(dims) - 1 - axis_at))
    return level


def normal_values(stream_key, shape, spread, most, cuts=(), kind=jnp.bfloat16):
    factor_of = block_levels(stream_key, shape, cuts, -0.22, 0.18) if cuts else 1.0
    values = jax.random.normal(stream_key, shape, jnp.float32) * spread * factor_of
    return jnp.minimum(jnp.maximum(values, -most), most).astype(kind)


def setup_inputs(seed: int = 0) -> dict:
    keys = jax.random.split(jax.random.key(seed), 9)
    return {
        "volume": normal_values(keys[0], (NZ, NH, W), 1.0, 6.0, ((0, 16), (1, 32))),
        "cotangent": normal_values(keys[1], (NZ, NH, W), 1.0, 6.0, ((0, 16), (1, 32)), jnp.float32),
        "kernel_in": normal_values(keys[2], (27, C), 27 ** -0.5, 1.25),
        "kernel_mid": normal_values(keys[3], (27, C, C), (27 * C) ** -0.5, 0.21875),
        "kernel_out": normal_values(keys[4], (27, C), (27 * C) ** -0.5, 0.21875),
        "measured": normal_values(keys[5], (NZ, ANG_ALL, BINS), 4.0, 24.0, ((0, 16),), jnp.float32),
        "angle_ids": draw_angle_ids(jax.random.fold_in(keys[8], 71), 0),
        "ray_bins": draw_ray_bins(jax.random.fold_in(keys[8], 71), 0),
    }


delta_scale = 6.0

def shifts():
    return [(step_z, step_y, step_x) for step_z in (-1, 0, 1) for step_y in (-1, 0, 1) for step_x in (-1, 0, 1)]

def pad_cells(field):
    return jnp.pad(field, ((0, 0), (1, 1), (1, 1), (1, 1)))

def window_at(padded, start_z, start_y, start_x, extent):
    return lax.slice(padded, (0, start_z, start_y, start_x), (padded.shape[0], start_z + extent[0], start_y + extent[1], start_x + extent[2]))

def forward_conv(padded, kernel, extent):
    summed = jnp.zeros((kernel.shape[1],) + tuple(extent), jnp.float32)
    for position, (step_z, step_y, step_x) in enumerate(shifts()):
        window = window_at(padded, 1 + step_z, 1 + step_y, 1 + step_x, extent)
        summed = summed + jnp.einsum('oc,czhw->ozhw', kernel[position].astype(jnp.float32), window.astype(jnp.float32))
    return summed

def adjoint_conv(padded, kernel, extent):
    summed = jnp.zeros((kernel.shape[2],) + tuple(extent), jnp.float32)
    for position, (step_z, step_y, step_x) in enumerate(shifts()):
        window = window_at(padded, 1 - step_z, 1 - step_y, 1 - step_x, extent)
        summed = summed + jnp.einsum('oc,ozhw->czhw', kernel[position].astype(jnp.float32), window.astype(jnp.float32))
    return summed

def kernel_grad(grad_out, padded_in, extent):
    pieces = []
    for position, (step_z, step_y, step_x) in enumerate(shifts()):
        window = window_at(padded_in, 1 + step_z, 1 + step_y, 1 + step_x, extent)
        pieces.append(jnp.einsum('ozhw,czhw->oc', grad_out.astype(jnp.float32), window.astype(jnp.float32)))
    return jnp.stack(pieces)

def silu_slope(value):
    sigma = jax.nn.sigmoid(value)
    return sigma * (1.0 + value * (1.0 - sigma))

def project_pair(first, second, ray_bins):
    slices = first.shape[0]
    flattened = jnp.concatenate((first.reshape(slices, -1), second.reshape(slices, -1)), axis=0).T

    def one_view(bins_view):
        return jax.ops.segment_sum(flattened, bins_view.reshape(-1), num_segments=BINS)
    per_view = lax.map(one_view, ray_bins)
    stacked = jnp.transpose(per_view, (2, 0, 1))
    return (stacked[:slices], stacked[slices:])

def back_project(rays, ray_bins):

    def accumulate(summed, view_pair):
        rays_view, bins_view = view_pair
        return (summed + jnp.take(rays_view, bins_view.reshape(-1), axis=1), None)
    initial = jnp.zeros((rays.shape[0], ray_bins.shape[1] * ray_bins.shape[2]), rays.dtype)
    summed = lax.scan(accumulate, initial, (jnp.transpose(rays, (1, 0, 2)), ray_bins))[0]
    return summed.reshape(rays.shape[0], ray_bins.shape[1], ray_bins.shape[2])

def curvature(residual):
    ratio = residual / delta_scale
    inner = 1.0 + ratio * ratio
    return 1.0 / (inner * jnp.sqrt(inner))

def reference(volume, cotangent, kernel_in, kernel_mid, kernel_out, measured, angle_ids, ray_bins):
    extent = volume.shape
    first_in = kernel_in[:, :, None]
    last_out = kernel_out[:, None, :]
    source_pad = pad_cells(volume[None])
    pre_first = forward_conv(source_pad, first_in, extent)
    act_first = jax.nn.silu(pre_first).astype(jnp.bfloat16)
    slope_first = silu_slope(pre_first)
    first_pad = pad_cells(act_first)
    pre_second = forward_conv(first_pad, kernel_mid, extent)
    act_second = jax.nn.silu(pre_second).astype(jnp.bfloat16)
    slope_second = silu_slope(pre_second)
    second_pad = pad_cells(act_second)
    residue = forward_conv(second_pad, last_out, extent)[0]
    denoised = volume.astype(jnp.float32) - residue
    chosen = jnp.take(measured, angle_ids, axis=1)
    forward_rays, cot_rays = project_pair(denoised, cotangent, ray_bins)
    weighted = curvature(forward_rays - chosen) * cot_rays
    grad_denoised = cotangent - 0.25 / ANG * back_project(weighted, ray_bins)
    grad_scale = float(NZ * NH * W) ** (-0.5)
    grad_last = (-grad_denoised)[None].astype(jnp.bfloat16)
    last_pad = pad_cells(grad_last)
    grad_kernel_out = kernel_grad(grad_last, second_pad, extent)[:, 0, :] * grad_scale
    grad_second = adjoint_conv(last_pad, last_out, extent)
    grad_mid = (grad_second * slope_second).astype(jnp.bfloat16)
    mid_pad = pad_cells(grad_mid)
    grad_kernel_mid = kernel_grad(grad_mid, first_pad, extent) * grad_scale
    grad_first = adjoint_conv(mid_pad, kernel_mid, extent)
    grad_low = (grad_first * slope_first).astype(jnp.bfloat16)
    low_pad = pad_cells(grad_low)
    grad_kernel_in = kernel_grad(grad_low, source_pad, extent)[:, :, 0] * grad_scale
    grad_volume = grad_denoised + adjoint_conv(low_pad, first_in, extent)[0]
    return (grad_volume, grad_kernel_in, grad_kernel_mid, grad_kernel_out)
```

```python
import functools

import jax
import jax.numpy as jnp
from jax import lax
from jax.experimental import pallas as pl
from jax.experimental.pallas import tpu as pltpu
from jax.sharding import PartitionSpec as P

BINS = 1024
ANG = 8
C = 32
W = 128
Z = 4
H = 4
HI = BINS // 128
TILES = ANG * Z

delta_scale = 6.0
F32 = jnp.float32
BF16 = jnp.bfloat16


def lanes_of(shape):
    return lax.broadcasted_iota(jnp.int32, shape, len(shape) - 1)


def from_left(x):
    lane = lanes_of(x.shape)
    return jnp.where(lane > 0, pltpu.roll(x, 1, x.ndim - 1), 0.0)


def from_right(x):
    lane = lanes_of(x.shape)
    return jnp.where(lane < W - 1, pltpu.roll(x, W - 1, x.ndim - 1), 0.0)


def dot(a, b):
    return jnp.dot(a, b, preferred_element_type=F32)


def dot_nt(a, b):
    return lax.dot_general(a, b, (((1,), (1,)), ((), ())), preferred_element_type=F32)


def row_ok(rows, first, count):
    at = lax.broadcasted_iota(jnp.int32, (rows, W), 0) // C + first
    return (at >= 0) & (at < count)


def banded(base, height, shift):
    rows = [pltpu.roll(base, h + shift, 1) if h + shift else base for h in range(height)]
    return jnp.concatenate(rows, axis=0)[:, :144].astype(BF16)


def triple(ref, z, start, size):
    return jnp.concatenate([ref[z + oz, start : start + size, :] for oz in range(3)], axis=0)


def three_shifts(ref, flat, count):
    shape = (count, 16, W)
    ref[:, 0:16, :] = from_left(flat).reshape(shape).astype(BF16)
    ref[:, 16:32, :] = flat.reshape(shape).astype(BF16)
    ref[:, 32:48, :] = from_right(flat).reshape(shape).astype(BF16)


def low_match(low_row):
    n = low_row.shape[1]
    at = lax.broadcasted_iota(jnp.int32, (128, n), 0)
    return jnp.where(low_row == at, 1.0, 0.0).astype(BF16)


def conv_mid(ref, weights, z, row):
    x = triple(ref, z, row * C, 3 * C)
    y = dot(weights, x)
    return y[C : 2 * C] + from_left(y[0:C]) + from_right(y[2 * C :])


def conv_last(ref, weights, z, row):
    y = dot(weights, triple(ref, z, row * C, 3 * C))
    return y[1:2] + from_left(y[0:1]) + from_right(y[2:3])


def project(field, bins_ref, a):
    parts, lows = [], []
    at = lax.broadcasted_iota(jnp.int32, (HI, W), 0)
    for h in range(H):
        bins = bins_ref[a, h : h + 1, :]
        match = (bins >> 7) == at
        rows = [jnp.where(match, field[h][r : r + 1, :], 0.0) for r in range(field[h].shape[0])]
        parts.append(jnp.concatenate(rows, axis=0))
        lows.append(low_match(bins & 127))
    part = jnp.concatenate(parts, axis=1)
    low = jnp.concatenate(lows, axis=1)
    head = part.astype(BF16)
    rest = (part - head.astype(F32)).astype(BF16)
    n = part.shape[0]
    both = dot_nt(jnp.concatenate([head, rest], axis=0), low)
    return both[:n] + both[n:]


def forward_kernel(depth_count, plane_count, pos, lo, mid, hi, first, second, third, cot, bins,
                   vc_out, act1_out, slope1_out, act2_out, slope2_out, rays_out,
                   vs, v3, vcs, a1, a2):
    depth_at = pos[0] * Z
    plane_at = pos[1] * H
    nz, nh = depth_count * Z, plane_count * H
    vs[...] = jnp.zeros_like(vs)
    vs[:, 0:4, :] = lo[...].astype(F32)
    vs[:, 4:8, :] = mid[...].astype(F32)
    vs[:, 8:12, :] = hi[...].astype(F32)
    three_shifts(v3, vs[...].reshape(12 * 16, W), 12)
    vcs[...] = jnp.zeros_like(vcs)
    for z in range(Z):
        for h in range(H):
            for oz in range(3):
                vcs[z * H + h, oz * 3 : oz * 3 + 3, :] = vs[z + 3 + oz, h + 3 : h + 6, :]
    vc_out[...] = vcs[...].astype(BF16)
    weights = banded(first[...], 10, 0)
    ok_rows = row_ok(10 * C, plane_at - 3, nh)
    for z in range(10):
        p = dot(weights, v3[z : z + 3].reshape(144, W))
        sigma = jax.nn.sigmoid(p)
        at = depth_at + (z - 3)
        ok = ok_rows & (at >= 0) & (at < nz)
        act = jnp.where(ok, p * sigma, 0.0).astype(BF16)
        a1[z] = act
        if 2 <= z < 8:
            act1_out[z - 2] = act[2 * C : 8 * C]
            slope1_out[z - 2] = (sigma * (1.0 + p * (1.0 - sigma)))[2 * C : 8 * C]
    wide = second[...]
    ok_rows = row_ok(8 * C, plane_at - 2, nh)
    for z in range(8):
        p = jnp.concatenate([conv_mid(a1, wide, z, h) for h in range(8)], axis=0)
        sigma = jax.nn.sigmoid(p)
        at = depth_at + (z - 2)
        ok = ok_rows & (at >= 0) & (at < nz)
        act = jnp.where(ok, p * sigma, 0.0).astype(BF16)
        slope2_out[z] = sigma * (1.0 + p * (1.0 - sigma))
        if 1 <= z < 7:
            a2[z - 1] = act[C : 7 * C]
            act2_out[z - 1] = act[C : 7 * C]
    last = third[...]
    field = []
    for h in range(H):
        rows = []
        for z in range(Z):
            rows.append(vs[z + 4, h + 4 : h + 5, :] - conv_last(a2, last, z, h))
        for z in range(Z):
            rows.append(cot[z, h : h + 1, :])
        field.append(jnp.concatenate(rows, axis=0))
    for a in range(ANG):
        tile = project(field, bins, a).reshape(2, Z, HI, 128)
        rays_out[a * Z : (a + 1) * Z, 0:HI, :] = tile[0]
        rays_out[a * Z : (a + 1) * Z, HI : 2 * HI, :] = tile[1]


def weigh_kernel(planes, rays, chosen, out):
    each = TILES // planes
    total = jnp.sum(rays[...], axis=0)
    for t in range(each):
        forward = total[t * 2 * HI : t * 2 * HI + HI]
        turned = total[t * 2 * HI + HI : (t + 1) * 2 * HI]
        ratio = (forward - chosen[t]) / delta_scale
        inner = 1.0 + ratio * ratio
        weighted = turned / (inner * jnp.sqrt(inner))
        out[:, t * HI : (t + 1) * HI, :] = jnp.broadcast_to(weighted[None], (planes, HI, 128))


def back_kernel(plane_count, pos, rays, bins_lo, bins_mid, bins_hi, cot_lo, cot_mid, cot_hi,
                slab_out, own_out, slab):
    plane_at = pos[1] * H
    nh = plane_count * H
    pieces = (bins_lo, bins_mid, bins_hi)
    cots = (cot_lo, cot_mid, cot_hi)
    at = lax.broadcasted_iota(jnp.int32, (HI, W), 0)
    spans = range(1, 11)
    total = [None] * len(spans)
    for a in range(ANG):
        rows = rays[a * Z : (a + 1) * Z].reshape(Z * HI, 128)
        head = rows.astype(BF16)
        rest = (rows - head.astype(F32)).astype(BF16)
        both = jnp.concatenate([head, rest], axis=0)
        bins = [pieces[h // H][a, h % H : h % H + 1, :] for h in spans]
        low = jnp.concatenate([low_match(b & 127) for b in bins], axis=1)
        spread = dot(both, low)
        spread = spread[: Z * HI] + spread[Z * HI :]
        for i, b in enumerate(bins):
            match = (b >> 7) == at
            match = jnp.concatenate([match] * Z, axis=0)
            term = jnp.where(match, spread[:, i * W : (i + 1) * W], 0.0)
            total[i] = term if total[i] is None else total[i] + term
    slab[...] = jnp.zeros_like(slab)
    for i, h in enumerate(spans):
        summed = jnp.sum(total[i].reshape(Z, HI, W), axis=1)
        field = cots[h // H][:, h % H, :] - (0.25 / ANG) * summed
        row = plane_at + h - H
        slab[h] = jnp.where((row >= 0) & (row < nh), -field, 0.0)
        if H <= h < 2 * H:
            own_out[h - H] = field
    slab_out[...] = slab[...].astype(BF16)


def backward_kernel(depth_count, plane_count, pos, lo, mid, hi, own, first, second, third,
                    vc, act1, slope1, act2, slope2,
                    volume_out, mid_out, out_out, in_out,
                    gs, v3, gx, gm, gm3, low, low3):
    depth_at = pos[0] * Z
    plane_at = pos[1] * H
    nz, nh = depth_count * Z, plane_count * H
    gs[...] = jnp.zeros_like(gs)
    for h in range(12):
        gs[0:3, h, :] = lo[h].astype(F32)[1:4]
        gs[3:7, h, :] = mid[h].astype(F32)
        gs[7:10, h, :] = hi[h].astype(F32)[0:3]
    three_shifts(v3, gs[...].reshape(160, W), 10)
    gx[...] = jnp.zeros_like(gx)
    rows = gs[3:7, 4:8, :].reshape(16, W)
    gx[:, 0, :] = from_right(rows)
    gx[:, 1, :] = rows
    gx[:, 2, :] = from_left(rows)
    weights = banded(third[...], 8, 1)
    ok_rows = row_ok(8 * C, plane_at - 2, nh)
    for z in range(8):
        y = dot(weights, v3[z : z + 3].reshape(144, W))
        at = depth_at + (z - 2)
        ok = ok_rows & (at >= 0) & (at < nz)
        g = jnp.where(ok, y * slope2[z], 0.0).astype(BF16)
        gm[z] = g
        if 2 <= z < 6:
            inner = g[2 * C : 6 * C].astype(F32)
            gm3[z - 2, 0] = from_right(inner).astype(BF16)
            gm3[z - 2, 1] = g[2 * C : 6 * C]
            gm3[z - 2, 2] = from_left(inner).astype(BF16)

    def shifted(ref):
        return jnp.concatenate(
            [
                jnp.concatenate([ref[z, ox, h * C : (h + 1) * C, :] for ox in range(3)], axis=0)
                for z in range(Z)
                for h in range(H)
            ],
            axis=1,
        )

    def windows(ref):
        return jnp.concatenate(
            [triple(ref, z, h * C, 3 * C) for z in range(Z) for h in range(H)], axis=1
        )

    mid_out[...] = dot_nt(shifted(gm3), windows(act1))
    gx_all = jnp.concatenate([gx[i] for i in range(16)], axis=1).astype(BF16)
    out_out[...] = dot_nt(gx_all, windows(act2))
    wide = second[...]
    ok_rows = row_ok(6 * C, plane_at - 1, nh)
    for z in range(6):
        y = jnp.concatenate([conv_mid(gm, wide, z, h) for h in range(6)], axis=0)
        at = depth_at + (z - 1)
        ok = ok_rows & (at >= 0) & (at < nz)
        g = jnp.where(ok, y * slope1[z], 0.0).astype(BF16)
        low[z] = g
        if 1 <= z < 5:
            inner = g[C : 5 * C].astype(F32)
            low3[z - 1, 0] = from_right(inner).astype(BF16)
            low3[z - 1, 1] = g[C : 5 * C]
            low3[z - 1, 2] = from_left(inner).astype(BF16)
    vc_all = jnp.concatenate([vc[i] for i in range(16)], axis=1)
    in_out[...] = dot_nt(vc_all, shifted(low3))
    last = first[...]
    for z in range(Z):
        for h in range(H):
            volume_out[z, h : h + 1, :] = own[h, z : z + 1, :] + conv_last(low, last, z, h)


def call(kernel, out_shapes, scratch, *args):
    specs = [pl.BlockSpec(memory_space=pltpu.VMEM) for _ in args]
    if args[0].dtype == jnp.int32 and args[0].ndim == 1:
        specs[0] = pl.BlockSpec(memory_space=pltpu.SMEM)
    return pl.pallas_call(
        kernel,
        out_shape=[jax.ShapeDtypeStruct(s, d) for s, d in out_shapes],
        in_specs=specs,
        out_specs=[pl.BlockSpec(memory_space=pltpu.VMEM) for _ in out_shapes],
        scratch_shapes=[pltpu.VMEM(s, d) for s, d in scratch],
        compiler_params=pltpu.CompilerParams(vmem_limit_bytes=40 * 1024 * 1024),
    )(*args)


def beside(cells, axis):
    count = lax.axis_size(axis)
    before = lax.ppermute(cells, axis, [(i, i + 1) for i in range(count - 1)])
    after = lax.ppermute(cells, axis, [(i + 1, i) for i in range(count - 1)])
    return before, after


def scatter_to(cells, axis):
    return lax.all_to_all(cells, axis, 0, 0, tiled=True)


def per_device(volume, cotangent, kernel_in, kernel_mid, kernel_out, measured, angle_ids, ray_bins):
    depths, planes = lax.axis_size("depth"), lax.axis_size("plane")
    depth_at, plane_at = lax.axis_index("depth"), lax.axis_index("plane")
    pos = jnp.stack([depth_at, plane_at]).astype(jnp.int32)

    v_before, v_after = beside(volume, "depth")
    tall = jnp.concatenate([v_before, volume, v_after], axis=0)
    t_before, t_after = beside(tall, "plane")

    in_k = kernel_in.reshape(3, 3, 3, C)
    mid_k = kernel_mid.reshape(3, 3, 3, C, C)
    out_k = kernel_out.reshape(3, 3, 3, C)
    flip = lambda k: k[::-1, ::-1, ::-1]

    def base(k):
        t = jnp.pad(jnp.transpose(k, (3, 0, 2, 1)), ((0, 0), (0, 0), (0, 0), (0, 13)))
        return jnp.pad(t.reshape(C, 144), ((0, 0), (0, 112))).astype(F32)

    def tail(k):
        t = jnp.transpose(k, (2, 0, 1, 3)).reshape(3, 9 * C)
        return jnp.pad(t, ((0, 13), (0, 0)))

    mid_forward = jnp.transpose(mid_k, (2, 3, 0, 1, 4)).reshape(3 * C, 9 * C)
    mid_back = jnp.transpose(flip(mid_k), (2, 4, 0, 1, 3)).reshape(3 * C, 9 * C)

    vc, act1, slope1, act2, slope2, rays = call(
        functools.partial(forward_kernel, depths, planes),
        [
            ((16, 16, W), BF16),
            ((6, 6 * C, W), BF16),
            ((6, 6 * C, W), F32),
            ((6, 6 * C, W), BF16),
            ((8, 8 * C, W), F32),
            ((TILES, 2 * HI, 128), F32),
        ],
        [
            ((12, 16, W), F32),
            ((12, 48, W), BF16),
            ((16, 16, W), F32),
            ((10, 10 * C, W), BF16),
            ((6, 6 * C, W), BF16),
        ],
        pos, t_before, tall, t_after, base(in_k), mid_forward, tail(out_k), cotangent, ray_bins,
    )
    each = TILES // planes
    gathered = scatter_to(rays.reshape(planes, each * 2 * HI, 128), "plane")
    tiles = plane_at * each + jnp.arange(each)
    chosen = jnp.stack(
        [
            lax.dynamic_slice(measured, (tiles[t] % Z, angle_ids[tiles[t] // Z], 0), (1, 1, BINS))
            for t in range(each)
        ]
    ).reshape(each, HI, 128)
    spread = call(
        functools.partial(weigh_kernel, planes),
        [((planes, each * HI, 128), F32)],
        [],
        gathered, chosen,
    )[0]
    weighted = scatter_to(spread, "plane").reshape(TILES, HI, 128)
    c_before, c_after = beside(cotangent, "plane")
    b_before, b_after = beside(ray_bins, "plane")
    slab, own = call(
        functools.partial(back_kernel, planes),
        [((12, Z, W), BF16), ((H, Z, W), F32)],
        [((12, Z, W), F32)],
        pos, weighted, b_before, ray_bins, b_after, c_before, cotangent, c_after,
    )
    s_before, s_after = beside(slab, "depth")
    grad_volume, term_mid, term_out, term_in = call(
        functools.partial(backward_kernel, depths, planes),
        [((Z, H, W), F32), ((3 * C, 9 * C), F32), ((16, 9 * C), F32), ((16, 3 * C), F32)],
        [
            ((10, 16, W), F32),
            ((10, 48, W), BF16),
            ((16, 16, W), F32),
            ((8, 8 * C, W), BF16),
            ((4, 3, 4 * C, W), BF16),
            ((6, 6 * C, W), BF16),
            ((4, 3, 4 * C, W), BF16),
        ],
        pos, s_before, slab, s_after, own, tail(flip(in_k)), mid_back, base(flip(out_k)),
        vc, act1, slope1, act2, slope2,
    )
    flat = jnp.concatenate(
        [term_mid.reshape(-1), term_out[:3].reshape(-1), term_in[:9].reshape(-1)]
    )
    used = flat.shape[0]
    room = 32 * 8 * 128
    sent = jnp.pad(flat, (0, room - used)).reshape(planes, room // planes // 128, 128)
    part = jnp.sum(scatter_to(sent, "plane"), axis=0)
    part = scatter_to(jnp.broadcast_to(part[None], (depths,) + part.shape), "depth")
    part = jnp.sum(part, axis=0)
    full = scatter_to(jnp.broadcast_to(part[None], (planes,) + part.shape), "plane").reshape(-1)
    cell_count = Z * depths * H * planes * W
    full = full * (float(cell_count) ** (-0.5))
    n_mid = 27 * C * C
    got_mid = full[:n_mid].reshape(3, C, 3, 3, C).transpose(2, 3, 0, 1, 4).reshape(27, C, C)
    got_out = full[n_mid : n_mid + 27 * C].reshape(3, 3, 3, C).transpose(1, 2, 0, 3).reshape(27, C)
    got_in = full[n_mid + 27 * C : used].reshape(27, C)
    return (grad_volume, got_in, got_mid, got_out)


def solution(mesh):
    placed = (
        P("depth", "plane", None),
        P("depth", "plane", None),
        P(),
        P(),
        P(),
        P("depth", None, None),
        P(),
        P(None, "plane", None),
    )
    return jax.shard_map(
        per_device,
        mesh=mesh,
        in_specs=placed,
        out_specs=(P("depth", "plane", None), P(), P(), P()),
        check_vma=False,
    )
```

```python
import functools

import jax
import jax.numpy as jnp
from jax import lax
from jax.experimental import pallas as pl
from jax.experimental.pallas import tpu as pltpu
from jax.sharding import PartitionSpec as P

BINS = 1024
ANG = 8
C = 32
W = 128
Z = 4
H = 4
HI = BINS // 128
TILES = ANG * Z

delta_scale = 6.0
F32 = jnp.float32
BF16 = jnp.bfloat16


def lanes_of(shape):
    return lax.broadcasted_iota(jnp.int32, shape, len(shape) - 1)


def from_left(x):
    lane = lanes_of(x.shape)
    return jnp.where(lane > 0, pltpu.roll(x, 1, x.ndim - 1), 0.0)


def from_right(x):
    lane = lanes_of(x.shape)
    return jnp.where(lane < W - 1, pltpu.roll(x, W - 1, x.ndim - 1), 0.0)


def dot(a, b):
    return jnp.dot(a, b, preferred_element_type=F32)


def dot_nt(a, b):
    return lax.dot_general(a, b, (((1,), (1,)), ((), ())), preferred_element_type=F32)


def row_ok(rows, first, count):
    at = lax.broadcasted_iota(jnp.int32, (rows, W), 0) // C + first
    return (at >= 0) & (at < count)


def banded(base, height, shift):
    rows = [pltpu.roll(base, h + shift, 1) if h + shift else base for h in range(height)]
    return jnp.concatenate(rows, axis=0)[:, :144].astype(BF16)


def triple(ref, z, start, size):
    return jnp.concatenate([ref[z + oz, start : start + size, :] for oz in range(3)], axis=0)


def three_shifts(ref, flat, count):
    shape = (count, 16, W)
    ref[:, 0:16, :] = from_left(flat).reshape(shape).astype(BF16)
    ref[:, 16:32, :] = flat.reshape(shape).astype(BF16)
    ref[:, 32:48, :] = from_right(flat).reshape(shape).astype(BF16)


def low_match(low_row):
    n = low_row.shape[1]
    at = lax.broadcasted_iota(jnp.int32, (128, n), 0).astype(low_row.dtype)
    return jnp.where(low_row == at, 1.0, 0.0).astype(BF16)


def conv_mid(ref, weights, z, row):
    x = triple(ref, z, row * C, 3 * C)
    y = dot(weights, x)
    return y[C : 2 * C] + from_left(y[0:C]) + from_right(y[2 * C :])


def conv_mid_back(ref, weights, z, row):
    x = jnp.concatenate(
        [
            ref[z + 2 - oz, (row + 2 - oy) * C : (row + 3 - oy) * C, :]
            for oz in range(3)
            for oy in range(3)
        ],
        axis=0,
    )
    y = dot(weights, x)
    return y[C : 2 * C] + from_right(y[0:C]) + from_left(y[2 * C :])


def conv_last(ref, weights, z, row):
    y = dot(weights, triple(ref, z, row * C, 3 * C))
    return y[1:2] + from_left(y[0:1]) + from_right(y[2:3])


def project(field, bins_ref, a):
    parts, lows = [], []
    at = lax.broadcasted_iota(jnp.int32, (HI, W), 0)
    for h in range(H):
        bins = bins_ref[a, h : h + 1, :]
        match = (bins >> 7) == at
        rows = [jnp.where(match, field[h][r : r + 1, :], 0.0) for r in range(field[h].shape[0])]
        parts.append(jnp.concatenate(rows, axis=0))
        lows.append(low_match(bins & 127))
    part = jnp.concatenate(parts, axis=1)
    low = jnp.concatenate(lows, axis=1)
    head = part.astype(BF16)
    rest = (part - head.astype(F32)).astype(BF16)
    n = part.shape[0]
    both = dot_nt(jnp.concatenate([head, rest], axis=0), low)
    return both[:n] + both[n:]


def pack_kernel(before, own, after, cot, bins, out):
    out[0:4] = before[...]
    out[4:8] = own[...]
    out[8:12] = after[...]
    head = cot[...].astype(BF16)
    out[12:16] = head
    out[16:20] = (cot[...] - head.astype(F32)).astype(BF16)
    out[20:28] = (bins[...] >> 7).astype(F32).astype(BF16)
    out[28:36] = (bins[...] & 127).astype(F32).astype(BF16)


def forward_kernel(depth_count, plane_count, pos, lo, mid, hi, first, second, third, cot, bins,
                   vc_out, act1_out, slope1_out, act2_out, slope2_out, rays_out,
                   vs, v3, vcs, a1, a2):
    depth_at = pos[0] * Z
    plane_at = pos[1] * H
    nz, nh = depth_count * Z, plane_count * H
    vs[...] = jnp.zeros_like(vs)
    vs[:, 0:4, :] = lo[0:12].astype(F32)
    vs[:, 4:8, :] = mid[0:12].astype(F32)
    vs[:, 8:12, :] = hi[0:12].astype(F32)
    three_shifts(v3, vs[...].reshape(12 * 16, W), 12)
    vcs[...] = jnp.zeros_like(vcs)
    for z in range(Z):
        for h in range(H):
            for oz in range(3):
                vcs[z * H + h, oz * 3 : oz * 3 + 3, :] = vs[z + 3 + oz, h + 3 : h + 6, :]
    vc_out[...] = vcs[...].astype(BF16)
    weights = banded(first[...], 10, 0)
    ok_rows = row_ok(10 * C, plane_at - 3, nh)
    for z in range(10):
        p = dot(weights, v3[z : z + 3].reshape(144, W))
        sigma = jax.nn.sigmoid(p)
        at = depth_at + (z - 3)
        ok = ok_rows & (at >= 0) & (at < nz)
        act = jnp.where(ok, p * sigma, 0.0).astype(BF16)
        a1[z] = act
        if 2 <= z < 8:
            act1_out[z - 2] = act[2 * C : 8 * C]
            slope1_out[z - 2] = (sigma * (1.0 + p * (1.0 - sigma)))[2 * C : 8 * C]
    wide = second[...]
    ok_rows = row_ok(8 * C, plane_at - 2, nh)
    for z in range(8):
        p = jnp.concatenate([conv_mid(a1, wide, z, h) for h in range(8)], axis=0)
        sigma = jax.nn.sigmoid(p)
        at = depth_at + (z - 2)
        ok = ok_rows & (at >= 0) & (at < nz)
        act = jnp.where(ok, p * sigma, 0.0).astype(BF16)
        slope2_out[z] = sigma * (1.0 + p * (1.0 - sigma))
        if 1 <= z < 7:
            a2[z - 1] = act[C : 7 * C]
            act2_out[z - 1] = act[C : 7 * C]
    last = third[...]
    field = []
    for h in range(H):
        rows = []
        for z in range(Z):
            rows.append(vs[z + 4, h + 4 : h + 5, :] - conv_last(a2, last, z, h))
        for z in range(Z):
            rows.append(cot[z, h : h + 1, :])
        field.append(jnp.concatenate(rows, axis=0))
    for a in range(ANG):
        tile = project(field, bins, a).reshape(2, Z, HI, 128)
        head = tile[0].astype(BF16).astype(F32)
        rows = jnp.concatenate([head, tile[0] - head, tile[1]], axis=1)
        rays_out[a * Z : (a + 1) * Z] = rows.astype(BF16)


def weigh_kernel(planes, rays, chosen, out):
    each = TILES // planes
    total = jnp.sum(rays[...].astype(F32), axis=0)
    for t in range(each):
        at = t * 3 * HI
        forward = total[at : at + HI] + total[at + HI : at + 2 * HI]
        turned = total[at + 2 * HI : at + 3 * HI]
        ratio = (forward - chosen[t]) / delta_scale
        inner = 1.0 + ratio * ratio
        weighted = turned / (inner * jnp.sqrt(inner))
        weighted = jnp.broadcast_to(weighted[None], (planes, HI, 128))
        out[:, t * HI : (t + 1) * HI, :] = weighted.astype(BF16)


def back_kernel(plane_count, pos, rays, lo, mid, hi, cot, slab_out, own_out, slab):
    plane_at = pos[1] * H
    nh = plane_count * H
    packs = [p[12:36].astype(F32) for p in (lo, mid, hi)]
    at = lax.broadcasted_iota(jnp.int32, (HI, W), 0).astype(F32)
    spans = range(1, 11)
    total = [None] * len(spans)
    for a in range(ANG):
        rows = rays[a * Z : (a + 1) * Z].astype(F32).reshape(Z * HI, 128).astype(BF16)
        highs = [packs[h // H][8 + a, h % H : h % H + 1, :] for h in spans]
        lows = [packs[h // H][16 + a, h % H : h % H + 1, :] for h in spans]
        spread = dot(rows, jnp.concatenate([low_match(b) for b in lows], axis=1))
        for i, b in enumerate(highs):
            match = jnp.concatenate([b == at] * Z, axis=0)
            term = jnp.where(match, spread[:, i * W : (i + 1) * W], 0.0)
            total[i] = term if total[i] is None else total[i] + term
    slab[...] = jnp.zeros_like(slab)
    for i, h in enumerate(spans):
        summed = jnp.sum(total[i].reshape(Z, HI, W), axis=1)
        if H <= h < 2 * H:
            rows = cot[:, h - H, :]
        else:
            pack = packs[h // H]
            rows = pack[0:4, h % H, :] + pack[4:8, h % H, :]
        field = rows - (0.25 / ANG) * summed
        row = plane_at + h - H
        slab[h] = jnp.where((row >= 0) & (row < nh), -field, 0.0)
        if H <= h < 2 * H:
            own_out[h - H] = field
    slab_out[...] = slab[...].astype(BF16)


def backward_kernel(depth_count, plane_count, pos, lo, mid, hi, own, first, second, third,
                    vc, act1, slope1, act2, slope2,
                    volume_out, terms_out,
                    gs, v3, gx, gm, gm3, low, low3, terms):
    depth_at = pos[0] * Z
    plane_at = pos[1] * H
    nz, nh = depth_count * Z, plane_count * H
    gs[...] = jnp.zeros_like(gs)
    for h in range(12):
        gs[0:3, h, :] = lo[h].astype(F32)[1:4]
        gs[3:7, h, :] = mid[h].astype(F32)
        gs[7:10, h, :] = hi[h].astype(F32)[0:3]
    three_shifts(v3, gs[...].reshape(160, W), 10)
    gx[...] = jnp.zeros_like(gx)
    rows = gs[3:7, 4:8, :].reshape(16, W)
    gx[:, 0, :] = from_right(rows)
    gx[:, 1, :] = rows
    gx[:, 2, :] = from_left(rows)
    weights = banded(third[...], 8, 1)
    ok_rows = row_ok(8 * C, plane_at - 2, nh)
    for z in range(8):
        y = dot(weights, v3[z : z + 3].reshape(144, W))
        at = depth_at + (z - 2)
        ok = ok_rows & (at >= 0) & (at < nz)
        g = jnp.where(ok, y * slope2[z], 0.0).astype(BF16)
        gm[z] = g
        if 2 <= z < 6:
            inner = g[2 * C : 6 * C].astype(F32)
            gm3[z - 2, 0] = from_right(inner).astype(BF16)
            gm3[z - 2, 1] = g[2 * C : 6 * C]
            gm3[z - 2, 2] = from_left(inner).astype(BF16)

    def shifted(ref):
        return jnp.concatenate(
            [
                jnp.concatenate([ref[z, ox, h * C : (h + 1) * C, :] for ox in range(3)], axis=0)
                for z in range(Z)
                for h in range(H)
            ],
            axis=1,
        )

    def windows(ref):
        rows = jnp.concatenate(
            [triple(ref, z, h * C, 3 * C) for z in range(Z) for h in range(H)], axis=1
        )
        return jnp.concatenate([rows, jnp.zeros((96, 16 * W), BF16)], axis=0)

    terms[...] = jnp.zeros_like(terms)
    term = dot_nt(shifted(gm3), windows(act1))
    terms[0:96] = term[:, 0:128]
    terms[96:192] = term[:, 128:256]
    tail = term[0:24, 256:384]
    for i in range(1, 4):
        tail = tail + pltpu.roll(term[24 * i : 24 * i + 24, 256:384], 32 * i, 1)
    terms[192:216] = tail
    gx_all = jnp.concatenate([gx[i] for i in range(16)], axis=1).astype(BF16)
    term = dot_nt(gx_all, windows(act2))
    for i in range(3):
        terms[216 + 3 * i : 219 + 3 * i] = term[0:3, 128 * i : 128 * i + 128]
    wide = second[...]
    ok_rows = row_ok(6 * C, plane_at - 1, nh)
    for z in range(6):
        y = jnp.concatenate([conv_mid_back(gm, wide, z, h) for h in range(6)], axis=0)
        at = depth_at + (z - 1)
        ok = ok_rows & (at >= 0) & (at < nz)
        g = jnp.where(ok, y * slope1[z], 0.0).astype(BF16)
        low[z] = g
        if 1 <= z < 5:
            inner = g[C : 5 * C].astype(F32)
            low3[z - 1, 0] = from_right(inner).astype(BF16)
            low3[z - 1, 1] = g[C : 5 * C]
            low3[z - 1, 2] = from_left(inner).astype(BF16)
    vc_all = jnp.concatenate([vc[i] for i in range(16)], axis=1)
    rows = jnp.concatenate([shifted(low3), jnp.zeros((32, 16 * W), BF16)], axis=0)
    terms[225:234] = dot_nt(vc_all, rows)[0:9]
    terms_out[...] = terms[...].reshape(terms_out.shape).astype(BF16)
    last = first[...]
    for z in range(Z):
        for h in range(H):
            volume_out[z, h : h + 1, :] = own[h, z : z + 1, :] + conv_last(low, last, z, h)


def unpack_kernel(scale, sums, in_out, mid_out, out_out):
    full = sums[...].astype(F32).reshape(256, 128) * scale
    quarters = [full] + [pltpu.roll(full, 128 - 32 * j, 1) for j in range(1, 4)]
    last = jnp.concatenate([q[192:216, 0:C] for q in quarters], axis=0)
    for q in range(9):
        for ox in range(3):
            if q < 8:
                start = 96 * (q // 4) + C * ox
                mid_out[q * 3 + ox] = quarters[q % 4][start : start + C, 0:C]
            else:
                mid_out[q * 3 + ox] = last[C * ox : C * ox + C]
        start = 216 + 3 * (q // 4)
        out_out[q * 3 : q * 3 + 3, :] = quarters[q % 4][start : start + 3, 0:C]
        for ox in range(3):
            in_out[q * 3 + ox : q * 3 + ox + 1, :] = quarters[ox][225 + q : 226 + q, 0:C]


def call(kernel, out_shapes, scratch, *args):
    specs = [pl.BlockSpec(memory_space=pltpu.VMEM) for _ in args]
    if args[0].dtype == jnp.int32 and args[0].ndim == 1:
        specs[0] = pl.BlockSpec(memory_space=pltpu.SMEM)
    return pl.pallas_call(
        kernel,
        out_shape=[jax.ShapeDtypeStruct(s, d) for s, d in out_shapes],
        in_specs=specs,
        out_specs=[pl.BlockSpec(memory_space=pltpu.VMEM) for _ in out_shapes],
        scratch_shapes=[pltpu.VMEM(s, d) for s, d in scratch],
        compiler_params=pltpu.CompilerParams(vmem_limit_bytes=40 * 1024 * 1024),
    )(*args)


def beside(cells, axis):
    count = lax.axis_size(axis)
    before = lax.ppermute(cells, axis, [(i, i + 1) for i in range(count - 1)])
    after = lax.ppermute(cells, axis, [(i + 1, i) for i in range(count - 1)])
    return before, after


def scatter_to(cells, axis):
    return lax.all_to_all(cells, axis, 0, 0, tiled=True)


def per_device(volume, cotangent, kernel_in, kernel_mid, kernel_out, measured, angle_ids, ray_bins):
    depths, planes = lax.axis_size("depth"), lax.axis_size("plane")
    depth_at, plane_at = lax.axis_index("depth"), lax.axis_index("plane")
    pos = jnp.stack([depth_at, plane_at]).astype(jnp.int32)

    v_before, v_after = beside(volume, "depth")
    pack = call(
        pack_kernel, [((36, H, W), BF16)], [], v_before, volume, v_after, cotangent, ray_bins
    )[0]
    p_before, p_after = beside(pack, "plane")

    in_k = kernel_in.reshape(3, 3, 3, C)
    mid_k = kernel_mid.reshape(3, 3, 3, C, C)
    out_k = kernel_out.reshape(3, 3, 3, C)
    flip = lambda k: k[::-1, ::-1, ::-1]

    def base(k):
        t = jnp.pad(jnp.transpose(k, (3, 0, 2, 1)), ((0, 0), (0, 0), (0, 0), (0, 13)))
        return jnp.pad(t.reshape(C, 144), ((0, 0), (0, 112))).astype(F32)

    def tail(k):
        t = jnp.transpose(k, (2, 0, 1, 3)).reshape(3, 9 * C)
        return jnp.pad(t, ((0, 13), (0, 0)))

    mid_forward = jnp.transpose(mid_k, (2, 3, 0, 1, 4)).reshape(3 * C, 9 * C)
    mid_back = jnp.transpose(mid_k, (2, 4, 0, 1, 3)).reshape(3 * C, 9 * C)

    vc, act1, slope1, act2, slope2, rays = call(
        functools.partial(forward_kernel, depths, planes),
        [
            ((16, 16, W), BF16),
            ((6, 6 * C, W), BF16),
            ((6, 6 * C, W), F32),
            ((6, 6 * C, W), BF16),
            ((8, 8 * C, W), F32),
            ((TILES, 3 * HI, 128), BF16),
        ],
        [
            ((12, 16, W), F32),
            ((12, 48, W), BF16),
            ((16, 16, W), F32),
            ((10, 10 * C, W), BF16),
            ((6, 6 * C, W), BF16),
        ],
        pos, p_before, pack, p_after, base(in_k), mid_forward, tail(out_k), cotangent, ray_bins,
    )
    each = TILES // planes
    gathered = scatter_to(rays.reshape(planes, each * 3 * HI, 128), "plane")
    tiles = plane_at * each + jnp.arange(each)
    chosen = jnp.stack(
        [
            lax.dynamic_slice(measured, (tiles[t] % Z, angle_ids[tiles[t] // Z], 0), (1, 1, BINS))
            for t in range(each)
        ]
    ).reshape(each, HI, 128)
    spread = call(
        functools.partial(weigh_kernel, planes),
        [((planes, each * HI, 128), BF16)],
        [],
        gathered, chosen,
    )[0]
    weighted = scatter_to(spread, "plane").reshape(TILES, HI, 128)
    slab, own = call(
        functools.partial(back_kernel, planes),
        [((12, Z, W), BF16), ((H, Z, W), F32)],
        [((12, Z, W), F32)],
        pos, weighted, p_before, pack, p_after, cotangent,
    )
    s_before, s_after = beside(slab, "depth")
    grad_volume, terms = call(
        functools.partial(backward_kernel, depths, planes),
        [((Z, H, W), F32), ((planes, 256 // planes, 128), BF16)],
        [
            ((10, 16, W), F32),
            ((10, 48, W), BF16),
            ((16, 16, W), F32),
            ((8, 8 * C, W), BF16),
            ((4, 3, 4 * C, W), BF16),
            ((6, 6 * C, W), BF16),
            ((4, 3, 4 * C, W), BF16),
            ((256, 128), F32),
        ],
        pos, s_before, slab, s_after, own, tail(flip(in_k)), mid_back, base(flip(out_k)),
        vc, act1, slope1, act2, slope2,
    )
    def shared(cells, axis):
        total = jnp.sum(cells.astype(F32), axis=0, keepdims=True).astype(BF16)
        return scatter_to(jnp.broadcast_to(total, (lax.axis_size(axis),) + total.shape[1:]), axis)

    sums = shared(shared(scatter_to(terms, "plane"), "depth"), "plane")
    cell_count = Z * depths * H * planes * W
    got_in, got_mid, got_out = call(
        functools.partial(unpack_kernel, float(cell_count) ** (-0.5)),
        [((27, C), F32), ((27, C, C), F32), ((27, C), F32)],
        [],
        sums,
    )
    return (grad_volume, got_in, got_mid, got_out)


def solution(mesh):
    placed = (
        P("depth", "plane", None),
        P("depth", "plane", None),
        P(),
        P(),
        P(),
        P("depth", None, None),
        P(),
        P(None, "plane", None),
    )
    return jax.shard_map(
        per_device,
        mesh=mesh,
        in_specs=placed,
        out_specs=(P("depth", "plane", None), P(), P(), P()),
        check_vma=False,
    )
```

```python
import functools

import jax
import jax.numpy as jnp
from jax import lax
from jax.experimental import pallas as pl
from jax.experimental.pallas import tpu as pltpu
from jax.sharding import Mesh
from jax.sharding import PartitionSpec as P

BINS = 1024
ANG = 8
C = 32
W = 128
Z = 4
H = 4
HI = BINS // 128
TILES = ANG * Z

delta_scale = 6.0

DEPTH = ("x", "z_hi")
PLANE = ("z_lo", "y", "core")
NEAR = ("x", "z_lo", "core")
FAR = ("z_hi", "y")
F32 = jnp.float32
BF16 = jnp.bfloat16


def lanes_of(shape):
    return lax.broadcasted_iota(jnp.int32, shape, len(shape) - 1)


def from_left(x):
    lane = lanes_of(x.shape)
    return jnp.where(lane > 0, pltpu.roll(x, 1, x.ndim - 1), 0.0)


def from_right(x):
    lane = lanes_of(x.shape)
    return jnp.where(lane < W - 1, pltpu.roll(x, W - 1, x.ndim - 1), 0.0)


def dot(a, b):
    return jnp.dot(a, b, preferred_element_type=F32)


def dot_nt(a, b):
    return lax.dot_general(a, b, (((1,), (1,)), ((), ())), preferred_element_type=F32)


def row_ok(rows, first, count):
    at = lax.broadcasted_iota(jnp.int32, (rows, W), 0) // C + first
    return (at >= 0) & (at < count)


def banded(base, height, shift):
    rows = [pltpu.roll(base, h + shift, 1) if h + shift else base for h in range(height)]
    return jnp.concatenate(rows, axis=0)[:, :144].astype(BF16)


def base_of(kernel, flip):
    lane = lanes_of((27, 256))
    oz, ox, oy = lane // 48, (lane % 48) // 16, lane % 16
    at = oz * 9 + oy * 3 + ox
    row = lax.broadcasted_iota(jnp.int32, (27, 256), 0)
    take = ((26 - at if flip else at) == row) & (oy < 3) & (lane < 144)
    take = jnp.where(take, 1.0, 0.0).astype(BF16)
    return lax.dot_general(kernel, take, (((0,), (0,)), ((), ())), preferred_element_type=F32)


def tail_of(kernel, flip):
    spot = lax.broadcasted_iota(jnp.int32, (C, 9 * C), 0)
    spread = jnp.where(lanes_of((C, 9 * C)) % C == spot, 1.0, 0.0).astype(BF16)
    wide = dot(kernel, spread)
    row = lax.broadcasted_iota(jnp.int32, (27, 9 * C), 0)
    row = 26 - row if flip else row
    wide = jnp.where(row // 3 == lanes_of((27, 9 * C)) // C, wide, 0.0).astype(BF16)
    lane = lanes_of((16, 27))
    lane = 26 - lane if flip else lane
    pick = lane % 3 == lax.broadcasted_iota(jnp.int32, (16, 27), 0)
    return dot(jnp.where(pick, 1.0, 0.0).astype(BF16), wide).astype(BF16)


def triple(ref, z, start, size):
    return jnp.concatenate([ref[z + oz, start : start + size, :] for oz in range(3)], axis=0)


def three_shifts(ref, flat, count):
    shape = (count, 16, W)
    ref[:, 0:16, :] = from_left(flat).reshape(shape).astype(BF16)
    ref[:, 16:32, :] = flat.reshape(shape).astype(BF16)
    ref[:, 32:48, :] = from_right(flat).reshape(shape).astype(BF16)


def low_match(low_row):
    n = low_row.shape[1]
    at = lax.broadcasted_iota(jnp.int32, (128, n), 0).astype(low_row.dtype)
    return jnp.where(low_row == at, 1.0, 0.0).astype(BF16)


def conv_mid(ref, weights, z, row):
    x = triple(ref, z, row * C, 3 * C)
    y = dot(weights, x)
    return y[C : 2 * C] + from_left(y[0:C]) + from_right(y[2 * C :])


def conv_mid_back(ref, weights, z, row):
    x = jnp.concatenate(
        [
            ref[z + 2 - oz, (row + 2 - oy) * C : (row + 3 - oy) * C, :]
            for oz in range(3)
            for oy in range(3)
        ],
        axis=0,
    )
    y = dot(weights, x)
    return y[C : 2 * C] + from_right(y[0:C]) + from_left(y[2 * C :])


def conv_last(ref, weights, z, row):
    y = dot(weights, triple(ref, z, row * C, 3 * C))
    return y[1:2] + from_left(y[0:1]) + from_right(y[2:3])


def project(field, bins_ref, a):
    parts, lows = [], []
    at = lax.broadcasted_iota(jnp.int32, (HI, W), 0)
    for h in range(H):
        bins = bins_ref[a, h : h + 1, :]
        match = (bins >> 7) == at
        rows = [jnp.where(match, field[h][r : r + 1, :], 0.0) for r in range(field[h].shape[0])]
        parts.append(jnp.concatenate(rows, axis=0))
        lows.append(low_match(bins & 127))
    part = jnp.concatenate(parts, axis=1)
    low = jnp.concatenate(lows, axis=1)
    head = part.astype(BF16)
    rest = (part - head.astype(F32)).astype(BF16)
    n = part.shape[0]
    both = dot_nt(jnp.concatenate([head, rest], axis=0), low)
    return both[:n] + both[n:]


def pack_kernel(before, own, after, cot, bins, out):
    out[0:4] = before[...]
    out[4:8] = own[...]
    out[8:12] = after[...]
    head = cot[...].astype(BF16)
    out[12:16] = head
    out[16:20] = (cot[...] - head.astype(F32)).astype(BF16)
    out[20:28] = (bins[...] >> 7).astype(F32).astype(BF16)
    out[28:36] = (bins[...] & 127).astype(F32).astype(BF16)


def forward_kernel(depth_count, plane_count, pos, lo, mid, hi, first, second, third, cot, bins,
                   vc_out, act1_out, slope1_out, act2_out, slope2_out, rays_out,
                   vs, v3, vcs, a1, a2):
    depth_at = pos[0] * Z
    plane_at = pos[1] * H
    nz, nh = depth_count * Z, plane_count * H
    vs[...] = jnp.zeros_like(vs)
    vs[:, 0:4, :] = lo[0:12].astype(F32)
    vs[:, 4:8, :] = mid[0:12].astype(F32)
    vs[:, 8:12, :] = hi[0:12].astype(F32)
    three_shifts(v3, vs[...].reshape(12 * 16, W), 12)
    vcs[...] = jnp.zeros_like(vcs)
    for z in range(8):
        for h in range(H):
            for oz in range(3):
                vcs[z * H + h, oz * 3 : oz * 3 + 3, :] = vs[z + 1 + oz, h + 3 : h + 6, :]
    vc_out[...] = vcs[...].astype(BF16)
    weights = banded(base_of(first[...], False), 10, 0)
    ok_rows = row_ok(10 * C, plane_at - 3, nh)
    for z in range(8):
        p = dot(weights, v3[z + 1 : z + 4].reshape(144, W))
        sigma = jax.nn.sigmoid(p)
        at = depth_at + (z - 2)
        ok = ok_rows & (at >= 0) & (at < nz)
        act = jnp.where(ok, p * sigma, 0.0).astype(BF16)
        a1[z] = act
        act1_out[z] = act[2 * C : 8 * C]
        slope1_out[z] = (sigma * (1.0 + p * (1.0 - sigma)))[2 * C : 8 * C]
    wide = jnp.concatenate(
        [jnp.concatenate([second[q * 3 + ox] for q in range(9)], axis=1) for ox in range(3)],
        axis=0,
    )
    ok_rows = row_ok(8 * C, plane_at - 2, nh)
    for z in range(6):
        p = jnp.concatenate([conv_mid(a1, wide, z, h) for h in range(8)], axis=0)
        sigma = jax.nn.sigmoid(p)
        at = depth_at + (z - 1)
        ok = ok_rows & (at >= 0) & (at < nz)
        act = jnp.where(ok, p * sigma, 0.0).astype(BF16)
        slope2_out[z] = sigma * (1.0 + p * (1.0 - sigma))
        a2[z] = act[C : 7 * C]
        act2_out[z] = act[C : 7 * C]
    last = tail_of(third[...], False)
    field = []
    for h in range(H):
        rows = []
        for z in range(Z):
            rows.append(vs[z + 4, h + 4 : h + 5, :] - conv_last(a2, last, z, h))
        for z in range(Z):
            rows.append(cot[z, h : h + 1, :])
        field.append(jnp.concatenate(rows, axis=0))
    for a in range(ANG):
        tile = project(field, bins, a).reshape(2, Z, HI, 128)
        head = tile[0].astype(BF16).astype(F32)
        rows = jnp.concatenate([head, tile[0] - head, tile[1]], axis=1)
        rays_out[a * Z : (a + 1) * Z] = rows.astype(BF16)


def weigh_kernel(planes, rays, chosen, out):
    each = TILES // planes
    total = jnp.sum(rays[...].astype(F32), axis=0)
    for t in range(each):
        at = t * 3 * HI
        forward = total[at : at + HI] + total[at + HI : at + 2 * HI]
        turned = total[at + 2 * HI : at + 3 * HI]
        ratio = (forward - chosen[t]) / delta_scale
        inner = 1.0 + ratio * ratio
        weighted = turned / (inner * jnp.sqrt(inner))
        weighted = jnp.broadcast_to(weighted[None], (planes, HI, 128))
        out[:, t * HI : (t + 1) * HI, :] = weighted.astype(BF16)


def back_kernel(plane_count, pos, rays, lo, mid, hi, cot, slab_out, own_out, slab):
    plane_at = pos[1] * H
    nh = plane_count * H
    packs = [p[12:36].astype(F32) for p in (lo, mid, hi)]
    at = lax.broadcasted_iota(jnp.int32, (HI, W), 0).astype(F32)
    spans = range(1, 11)
    total = [None] * len(spans)
    for a in range(ANG):
        rows = rays[a * Z : (a + 1) * Z].astype(F32).reshape(Z * HI, 128).astype(BF16)
        highs = [packs[h // H][8 + a, h % H : h % H + 1, :] for h in spans]
        lows = [packs[h // H][16 + a, h % H : h % H + 1, :] for h in spans]
        spread = dot(rows, jnp.concatenate([low_match(b) for b in lows], axis=1))
        for i, b in enumerate(highs):
            match = jnp.concatenate([b == at] * Z, axis=0)
            term = jnp.where(match, spread[:, i * W : (i + 1) * W], 0.0)
            total[i] = term if total[i] is None else total[i] + term
    slab[...] = jnp.zeros_like(slab)
    for i, h in enumerate(spans):
        summed = jnp.sum(total[i].reshape(Z, HI, W), axis=1)
        if H <= h < 2 * H:
            rows = cot[:, h - H, :]
        else:
            pack = packs[h // H]
            rows = pack[0:4, h % H, :] + pack[4:8, h % H, :]
        field = rows - (0.25 / ANG) * summed
        row = plane_at + h - H
        slab[h] = jnp.where((row >= 0) & (row < nh), -field, 0.0)
        if H <= h < 2 * H:
            own_out[h - H] = field
    slab_out[...] = slab[...].astype(BF16)


def backward_kernel(depth_count, plane_count, pos, slab, own, first, second, third,
                    vc, act1, slope1, act2, slope2,
                    volume_out, before_out, after_out, terms_out,
                    gs, v3, gx, gm, gm3, low, low3, terms):
    depth_at = pos[0] * Z
    plane_at = pos[1] * H
    nz, nh = depth_count * Z, plane_count * H
    gs[...] = jnp.zeros_like(gs)
    for h in range(12):
        gs[2:6, h, :] = slab[h].astype(F32)
    three_shifts(v3, gs[...].reshape(128, W), 8)
    gx[...] = jnp.zeros_like(gx)
    rows = gs[2:6, 4:8, :].reshape(16, W)
    gx[:, 0, :] = from_right(rows)
    gx[:, 1, :] = rows
    gx[:, 2, :] = from_left(rows)
    edge = jnp.zeros((2, 8 * C, W), BF16)
    gm[0:2] = edge
    gm[8:10] = edge
    edge = jnp.zeros((2, 6 * C, W), BF16)
    low[0:2] = edge
    low[10:12] = edge
    weights = banded(base_of(third[...], True), 8, 1)
    ok_rows = row_ok(8 * C, plane_at - 2, nh)
    for z in range(6):
        y = dot(weights, v3[z : z + 3].reshape(144, W))
        at = depth_at + (z - 1)
        ok = ok_rows & (at >= 0) & (at < nz)
        g = jnp.where(ok, y * slope2[z], 0.0).astype(BF16)
        gm[z + 2] = g
        inner = g[2 * C : 6 * C].astype(F32)
        gm3[z, 0] = from_right(inner).astype(BF16)
        gm3[z, 1] = g[2 * C : 6 * C]
        gm3[z, 2] = from_left(inner).astype(BF16)

    def shifted(ref, slices):
        return jnp.concatenate(
            [
                jnp.concatenate([ref[z, ox, h * C : (h + 1) * C, :] for ox in range(3)], axis=0)
                for z in range(slices)
                for h in range(H)
            ],
            axis=1,
        )

    def windows(ref, slices):
        rows = jnp.concatenate(
            [triple(ref, z, h * C, 3 * C) for z in range(slices) for h in range(H)], axis=1
        )
        return jnp.concatenate([rows, jnp.zeros((96, slices * H * W), BF16)], axis=0)

    terms[...] = jnp.zeros_like(terms)
    term = dot_nt(shifted(gm3, 6), windows(act1, 6))
    terms[0:96] = term[:, 0:128]
    terms[96:192] = term[:, 128:256]
    tail = term[0:24, 256:384]
    for i in range(1, 4):
        tail = tail + pltpu.roll(term[24 * i : 24 * i + 24, 256:384], 32 * i, 1)
    terms[192:216] = tail
    gx_all = jnp.concatenate([gx[i] for i in range(16)], axis=1).astype(BF16)
    term = dot_nt(gx_all, windows(act2, 4))
    for i in range(3):
        terms[216 + 3 * i : 219 + 3 * i] = term[0:3, 128 * i : 128 * i + 128]
    wide = second[...]
    ok_rows = row_ok(6 * C, plane_at - 1, nh)
    for z in range(8):
        y = jnp.concatenate([conv_mid_back(gm, wide, z, h) for h in range(6)], axis=0)
        at = depth_at + (z - 2)
        ok = ok_rows & (at >= 0) & (at < nz)
        g = jnp.where(ok, y * slope1[z], 0.0).astype(BF16)
        low[z + 2] = g
        inner = g[C : 5 * C].astype(F32)
        low3[z, 0] = from_right(inner).astype(BF16)
        low3[z, 1] = g[C : 5 * C]
        low3[z, 2] = from_left(inner).astype(BF16)
    vc_all = jnp.concatenate([vc[i] for i in range(32)], axis=1)
    rows = jnp.concatenate([shifted(low3, 8), jnp.zeros((32, 32 * W), BF16)], axis=0)
    terms[225:234] = dot_nt(vc_all, rows)[0:9]
    terms_out[...] = terms[...].reshape(terms_out.shape).astype(BF16)
    last = tail_of(first[...], True)
    for z in range(10):
        for h in range(H):
            row = conv_last(low, last, z, h)
            if z < 3:
                before_out[z, h : h + 1, :] = row
            elif z < 7:
                volume_out[z - 3, h : h + 1, :] = own[h, z - 3 : z - 2, :] + row
            else:
                after_out[z - 7, h : h + 1, :] = row


def sum_kernel(sums, out):
    total = jnp.sum(sums[...].astype(F32), axis=0, keepdims=True)
    out[...] = jnp.broadcast_to(total, out.shape).astype(BF16)


def unpack_kernel(scale, sums, volume, before, after, volume_out, in_out, mid_out, out_out):
    volume_out[0] = volume[0] + before[0]
    volume_out[1:3] = volume[1:3] + before[1:3] + after[0:2]
    volume_out[3] = volume[3] + after[2]
    full = sums[...].astype(F32).reshape(256, 128) * scale
    quarters = [full] + [pltpu.roll(full, 128 - 32 * j, 1) for j in range(1, 4)]
    last = jnp.concatenate([q[192:216, 0:C] for q in quarters], axis=0)
    for q in range(9):
        for ox in range(3):
            if q < 8:
                start = 96 * (q // 4) + C * ox
                mid_out[q * 3 + ox] = quarters[q % 4][start : start + C, 0:C]
            else:
                mid_out[q * 3 + ox] = last[C * ox : C * ox + C]
        start = 216 + 3 * (q // 4)
        out_out[q * 3 : q * 3 + 3, :] = quarters[q % 4][start : start + 3, 0:C]
        for ox in range(3):
            in_out[q * 3 + ox : q * 3 + ox + 1, :] = quarters[ox][225 + q : 226 + q, 0:C]


def call(kernel, out_shapes, scratch, *args):
    specs = [pl.BlockSpec(memory_space=pltpu.VMEM) for _ in args]
    if args[0].dtype == jnp.int32 and args[0].ndim == 1:
        specs[0] = pl.BlockSpec(memory_space=pltpu.SMEM)
    return pl.pallas_call(
        kernel,
        out_shape=[jax.ShapeDtypeStruct(s, d) for s, d in out_shapes],
        in_specs=specs,
        out_specs=[pl.BlockSpec(memory_space=pltpu.VMEM) for _ in out_shapes],
        scratch_shapes=[pltpu.VMEM(s, d) for s, d in scratch],
        compiler_params=pltpu.CompilerParams(vmem_limit_bytes=40 * 1024 * 1024),
    )(*args)


def beside(cells, axis):
    count = lax.axis_size(axis)
    before = lax.ppermute(cells, axis, [(i, i + 1) for i in range(count - 1)])
    after = lax.ppermute(cells, axis, [(i + 1, i) for i in range(count - 1)])
    return before, after


def scatter_to(cells, axis):
    return lax.all_to_all(cells, axis, 0, 0, tiled=True)


def per_device(volume, cotangent, kernel_in, kernel_mid, kernel_out, measured, angle_ids, ray_bins):
    depths, planes = lax.axis_size(DEPTH), lax.axis_size(PLANE)
    near, far = lax.axis_size(NEAR), lax.axis_size(FAR)
    depth_at, plane_at = lax.axis_index(DEPTH), lax.axis_index(PLANE)
    pos = jnp.stack([depth_at, plane_at]).astype(jnp.int32)

    v_before, v_after = beside(volume, DEPTH)
    pack = call(
        pack_kernel, [((36, H, W), BF16)], [], v_before, volume, v_after, cotangent, ray_bins
    )[0]
    p_before, p_after = beside(pack, PLANE)

    mid_back = jnp.transpose(kernel_mid.reshape(3, 3, 3, C, C), (2, 4, 0, 1, 3))
    mid_back = mid_back.reshape(3 * C, 9 * C)

    vc, act1, slope1, act2, slope2, rays = call(
        functools.partial(forward_kernel, depths, planes),
        [
            ((32, 16, W), BF16),
            ((8, 6 * C, W), BF16),
            ((8, 6 * C, W), F32),
            ((6, 6 * C, W), BF16),
            ((6, 8 * C, W), F32),
            ((TILES, 3 * HI, 128), BF16),
        ],
        [
            ((12, 16, W), F32),
            ((12, 48, W), BF16),
            ((32, 16, W), F32),
            ((8, 10 * C, W), BF16),
            ((6, 6 * C, W), BF16),
        ],
        pos, p_before, pack, p_after, kernel_in, kernel_mid, kernel_out, cotangent, ray_bins,
    )
    each = TILES // planes
    gathered = scatter_to(rays.reshape(planes, each * 3 * HI, 128), PLANE)
    tiles = plane_at * each + jnp.arange(each)
    chosen = jnp.stack(
        [
            lax.dynamic_slice(measured, (tiles[t] % Z, angle_ids[tiles[t] // Z], 0), (1, 1, BINS))
            for t in range(each)
        ]
    ).reshape(each, HI, 128)
    spread = call(
        functools.partial(weigh_kernel, planes),
        [((planes, each * HI, 128), BF16)],
        [],
        gathered, chosen,
    )[0]
    weighted = scatter_to(spread, PLANE).reshape(TILES, HI, 128)
    slab, own = call(
        functools.partial(back_kernel, planes),
        [((12, Z, W), BF16), ((H, Z, W), F32)],
        [((12, Z, W), F32)],
        pos, weighted, p_before, pack, p_after, cotangent,
    )
    partial, before, after, terms = call(
        functools.partial(backward_kernel, depths, planes),
        [
            ((Z, H, W), F32),
            ((3, H, W), F32),
            ((3, H, W), F32),
            ((near, 256 // near, 128), BF16),
        ],
        [
            ((8, 16, W), F32),
            ((8, 48, W), BF16),
            ((16, 16, W), F32),
            ((10, 8 * C, W), BF16),
            ((6, 3, 4 * C, W), BF16),
            ((12, 6 * C, W), BF16),
            ((8, 3, 4 * C, W), BF16),
            ((256, 128), F32),
        ],
        pos, slab, own, kernel_in, mid_back, kernel_out, vc, act1, slope1, act2, slope2,
    )
    got_before = lax.ppermute(after, DEPTH, [(i, i + 1) for i in range(depths - 1)])
    got_after = lax.ppermute(before, DEPTH, [(i + 1, i) for i in range(depths - 1)])

    def spread_sum(cells, count):
        return call(sum_kernel, [((count,) + cells.shape[1:], BF16)], [], cells)[0]

    sums = scatter_to(terms, NEAR)
    sums = scatter_to(spread_sum(sums, far), FAR)
    sums = scatter_to(spread_sum(sums, near), NEAR)
    cell_count = Z * depths * H * planes * W
    grad_volume, got_in, got_mid, got_out = call(
        functools.partial(unpack_kernel, float(cell_count) ** (-0.5)),
        [((Z, H, W), F32), ((27, C), F32), ((27, C, C), F32), ((27, C), F32)],
        [],
        sums, partial, got_before, got_after,
    )
    return (grad_volume, got_in, got_mid, got_out)


def solution(mesh):
    depths, planes = mesh.devices.shape
    x = 4 if depths % 16 == 0 else 2
    fine = Mesh(
        mesh.devices.reshape(x, depths // x, 2, planes // 4, 2), DEPTH + PLANE
    )
    placed = (
        P(DEPTH, PLANE, None),
        P(DEPTH, PLANE, None),
        P(),
        P(),
        P(),
        P(DEPTH, None, None),
        P(),
        P(None, PLANE, None),
    )
    return jax.shard_map(
        per_device,
        mesh=fine,
        in_specs=placed,
        out_specs=(P(DEPTH, PLANE, None), P(), P(), P()),
        check_vma=False,
    )
```

```python
import functools

import jax
import jax.numpy as jnp
from jax import lax
from jax.experimental import pallas as pl
from jax.experimental.pallas import tpu as pltpu
from jax.sharding import PartitionSpec as P

BINS = 1024
ANG = 8
C = 32
W = 128
Z = 4
H = 4
HI = BINS // 128
TILES = ANG * Z

delta_scale = 6.0

DEPTH = "depth"
PLANE = "plane"
F32 = jnp.float32
BF16 = jnp.bfloat16


def lanes_of(shape):
    return lax.broadcasted_iota(jnp.int32, shape, len(shape) - 1)


def from_left(x):
    lane = lanes_of(x.shape)
    return jnp.where(lane > 0, pltpu.roll(x, 1, x.ndim - 1), 0.0)


def from_right(x):
    lane = lanes_of(x.shape)
    return jnp.where(lane < W - 1, pltpu.roll(x, W - 1, x.ndim - 1), 0.0)


def dot(a, b):
    return jnp.dot(a, b, preferred_element_type=F32)


def dot_nt(a, b):
    return lax.dot_general(a, b, (((1,), (1,)), ((), ())), preferred_element_type=F32)


def row_ok(rows, first, count):
    at = lax.broadcasted_iota(jnp.int32, (rows, W), 0) // C + first
    return (at >= 0) & (at < count)


def banded(base, height, shift):
    rows = [pltpu.roll(base, h + shift, 1) if h + shift else base for h in range(height)]
    return jnp.concatenate(rows, axis=0)[:, :144].astype(BF16)


def base_of(kernel, flip):
    lane = lanes_of((27, 256))
    oz, ox, oy = lane // 48, (lane % 48) // 16, lane % 16
    at = oz * 9 + oy * 3 + ox
    row = lax.broadcasted_iota(jnp.int32, (27, 256), 0)
    take = ((26 - at if flip else at) == row) & (oy < 3) & (lane < 144)
    take = jnp.where(take, 1.0, 0.0).astype(BF16)
    return lax.dot_general(kernel, take, (((0,), (0,)), ((), ())), preferred_element_type=F32)


def tail_of(kernel, flip):
    spot = lax.broadcasted_iota(jnp.int32, (C, 9 * C), 0)
    spread = jnp.where(lanes_of((C, 9 * C)) % C == spot, 1.0, 0.0).astype(BF16)
    wide = dot(kernel, spread)
    row = lax.broadcasted_iota(jnp.int32, (27, 9 * C), 0)
    row = 26 - row if flip else row
    wide = jnp.where(row // 3 == lanes_of((27, 9 * C)) // C, wide, 0.0).astype(BF16)
    lane = lanes_of((16, 27))
    lane = 26 - lane if flip else lane
    pick = lane % 3 == lax.broadcasted_iota(jnp.int32, (16, 27), 0)
    return dot(jnp.where(pick, 1.0, 0.0).astype(BF16), wide).astype(BF16)


def triple(ref, z, start, size):
    return jnp.concatenate([ref[z + oz, start : start + size, :] for oz in range(3)], axis=0)


def three_shifts(ref, flat, count):
    shape = (count, 16, W)
    ref[:, 0:16, :] = from_left(flat).reshape(shape).astype(BF16)
    ref[:, 16:32, :] = flat.reshape(shape).astype(BF16)
    ref[:, 32:48, :] = from_right(flat).reshape(shape).astype(BF16)


def low_match(low_row):
    n = low_row.shape[1]
    at = lax.broadcasted_iota(jnp.int32, (128, n), 0).astype(low_row.dtype)
    return jnp.where(low_row == at, 1.0, 0.0).astype(BF16)


def conv_mid(ref, weights, z, row):
    x = triple(ref, z, row * C, 3 * C)
    y = dot(weights, x)
    return y[C : 2 * C] + from_left(y[0:C]) + from_right(y[2 * C :])


def conv_mid_back(ref, weights, z, row):
    x = jnp.concatenate(
        [
            ref[z + 2 - oz, (row + 2 - oy) * C : (row + 3 - oy) * C, :]
            for oz in range(3)
            for oy in range(3)
        ],
        axis=0,
    )
    y = dot(weights, x)
    return y[C : 2 * C] + from_right(y[0:C]) + from_left(y[2 * C :])


def conv_last(ref, weights, z, row):
    y = dot(weights, triple(ref, z, row * C, 3 * C))
    return y[1:2] + from_left(y[0:1]) + from_right(y[2:3])


def project(field, bins_ref, a):
    parts, lows = [], []
    at = lax.broadcasted_iota(jnp.int32, (HI, W), 0)
    for h in range(H):
        bins = bins_ref[a, h : h + 1, :]
        match = (bins >> 7) == at
        rows = [jnp.where(match, field[h][r : r + 1, :], 0.0) for r in range(field[h].shape[0])]
        parts.append(jnp.concatenate(rows, axis=0))
        lows.append(low_match(bins & 127))
    part = jnp.concatenate(parts, axis=1)
    low = jnp.concatenate(lows, axis=1)
    head = part.astype(BF16)
    rest = (part - head.astype(F32)).astype(BF16)
    n = part.shape[0]
    both = dot_nt(jnp.concatenate([head, rest], axis=0), low)
    return both[:n] + both[n:]


def weights_kernel(first, second, third, first_out, wide_out, last_out,
                   first_back, wide_back, last_back):
    first_out[...] = banded(base_of(first[...], False), 10, 0)
    first_back[...] = banded(base_of(third[...], True), 8, 1)
    last_out[...] = tail_of(third[...], False)
    last_back[...] = tail_of(first[...], True)
    for ox in range(3):
        blocks = [second[q * 3 + ox] for q in range(9)]
        wide_out[ox * C : (ox + 1) * C, :] = jnp.concatenate(blocks, axis=1)
        blocks = jnp.concatenate(blocks, axis=0).astype(F32)
        wide_back[ox * C : (ox + 1) * C, :] = blocks.T.astype(BF16)


def near_slot(pos, count, slots, step):
    at = pos[0] + step
    rows = slots[jnp.clip(at, 0, count - 1)].astype(F32)
    return jnp.where((at >= 0) & (at < count), rows, 0.0)


def in_order(at, first, second):
    even = (at & 1) == 0
    return jnp.where(even, second, first), jnp.where(even, first, second)


def pack_kernel(pos, first, second, own, cot, bins, out):
    before, after = in_order(pos[0], first[...].astype(F32), second[...].astype(F32))
    out[0:4] = before.astype(BF16)
    out[4:8] = own[...]
    out[8:12] = after.astype(BF16)
    head = cot[...].astype(BF16)
    out[12:16] = head
    out[16:20] = (cot[...] - head.astype(F32)).astype(BF16)
    out[20:28] = (bins[...] >> 7).astype(F32).astype(BF16)
    out[28:36] = (bins[...] & 127).astype(F32).astype(BF16)


def forward_kernel(depth_count, plane_count, pos, swap_a, swap_b, mid, first, second, third, cot, bins,
                   vc_out, act1_out, slope1_out, act2_out, slope2_out, rays_out,
                   vs, v3, vcs, a1, a2):
    depth_at = pos[0] * Z
    plane_at = pos[1] * H
    nz, nh = depth_count * Z, plane_count * H
    vs[...] = jnp.zeros_like(vs)
    lo, hi = in_order(pos[1], swap_a[0:12].astype(F32), swap_b[0:12].astype(F32))
    vs[:, 0:4, :] = lo
    vs[:, 4:8, :] = mid[0:12].astype(F32)
    vs[:, 8:12, :] = hi
    three_shifts(v3, vs[...].reshape(12 * 16, W), 12)
    vcs[...] = jnp.zeros_like(vcs)
    for z in range(8):
        for h in range(H):
            for oz in range(3):
                vcs[z * H + h, oz * 3 : oz * 3 + 3, :] = vs[z + 1 + oz, h + 3 : h + 6, :]
    vc_out[...] = vcs[...].astype(BF16)
    weights = first[...]
    ok_rows = row_ok(10 * C, plane_at - 3, nh)
    for z in range(8):
        p = dot(weights, v3[z + 1 : z + 4].reshape(144, W))
        sigma = jax.nn.sigmoid(p)
        at = depth_at + (z - 2)
        ok = ok_rows & (at >= 0) & (at < nz)
        act = jnp.where(ok, p * sigma, 0.0).astype(BF16)
        a1[z] = act
        act1_out[z] = act[2 * C : 8 * C]
        slope1_out[z] = (sigma * (1.0 + p * (1.0 - sigma)))[2 * C : 8 * C]
    wide = second[...]
    ok_rows = row_ok(8 * C, plane_at - 2, nh)
    for z in range(6):
        p = jnp.concatenate([conv_mid(a1, wide, z, h) for h in range(8)], axis=0)
        sigma = jax.nn.sigmoid(p)
        at = depth_at + (z - 1)
        ok = ok_rows & (at >= 0) & (at < nz)
        act = jnp.where(ok, p * sigma, 0.0).astype(BF16)
        slope2_out[z] = sigma * (1.0 + p * (1.0 - sigma))
        a2[z] = act[C : 7 * C]
        act2_out[z] = act[C : 7 * C]
    last = third[...]
    field = []
    for h in range(H):
        rows = []
        for z in range(Z):
            rows.append(vs[z + 4, h + 4 : h + 5, :] - conv_last(a2, last, z, h))
        for z in range(Z):
            rows.append(cot[z, h : h + 1, :])
        field.append(jnp.concatenate(rows, axis=0))
    for a in range(ANG):
        tile = project(field, bins, a).reshape(2, Z, HI, 128)
        head = tile[0].astype(BF16).astype(F32)
        rows = jnp.concatenate([head, tile[0] - head, tile[1]], axis=1)
        rays_out[a * Z : (a + 1) * Z] = rows.astype(BF16)


def weigh_kernel(planes, rays, chosen, out):
    each = TILES // planes
    total = jnp.sum(rays[...].astype(F32), axis=0)
    for t in range(each):
        at = t * 3 * HI
        forward = total[at : at + HI] + total[at + HI : at + 2 * HI]
        turned = total[at + 2 * HI : at + 3 * HI]
        ratio = (forward - chosen[t]) / delta_scale
        inner = 1.0 + ratio * ratio
        weighted = turned / (inner * jnp.sqrt(inner))
        weighted = jnp.broadcast_to(weighted[None], (planes, HI, 128))
        out[:, t * HI : (t + 1) * HI, :] = weighted.astype(BF16)


def back_kernel(plane_count, pos, rays, swap_a, swap_b, mid, cot, slab_out, own_out, slab):
    plane_at = pos[1] * H
    nh = plane_count * H
    lo, hi = in_order(pos[1], swap_a[12:36].astype(F32), swap_b[12:36].astype(F32))
    packs = [lo, mid[12:36].astype(F32), hi]
    at = lax.broadcasted_iota(jnp.int32, (HI, W), 0).astype(F32)
    spans = range(1, 11)
    total = [None] * len(spans)
    for a in range(ANG):
        rows = rays[a * Z : (a + 1) * Z].astype(F32).reshape(Z * HI, 128).astype(BF16)
        highs = [packs[h // H][8 + a, h % H : h % H + 1, :] for h in spans]
        lows = [packs[h // H][16 + a, h % H : h % H + 1, :] for h in spans]
        spread = dot(rows, jnp.concatenate([low_match(b) for b in lows], axis=1))
        for i, b in enumerate(highs):
            match = jnp.concatenate([b == at] * Z, axis=0)
            term = jnp.where(match, spread[:, i * W : (i + 1) * W], 0.0)
            total[i] = term if total[i] is None else total[i] + term
    slab[...] = jnp.zeros_like(slab)
    for i, h in enumerate(spans):
        summed = jnp.sum(total[i].reshape(Z, HI, W), axis=1)
        if H <= h < 2 * H:
            rows = cot[:, h - H, :]
        else:
            pack = packs[h // H]
            rows = pack[0:4, h % H, :] + pack[4:8, h % H, :]
        field = rows - (0.25 / ANG) * summed
        row = plane_at + h - H
        slab[h] = jnp.where((row >= 0) & (row < nh), -field, 0.0)
        if H <= h < 2 * H:
            own_out[h - H] = field
    slab_out[...] = slab[...].astype(BF16)


def backward_kernel(depth_count, plane_count, pos, slab, own, first, second, third,
                    vc, act1, slope1, act2, slope2,
                    volume_out, terms_out,
                    gs, v3, gx, gm, gm3, low, low3, terms, side):
    depth_at = pos[0] * Z
    plane_at = pos[1] * H
    nz, nh = depth_count * Z, plane_count * H
    gs[...] = jnp.zeros_like(gs)
    for h in range(12):
        gs[2:6, h, :] = slab[h].astype(F32)
    three_shifts(v3, gs[...].reshape(128, W), 8)
    gx[...] = jnp.zeros_like(gx)
    rows = gs[2:6, 4:8, :].reshape(16, W)
    gx[:, 0, :] = from_right(rows)
    gx[:, 1, :] = rows
    gx[:, 2, :] = from_left(rows)
    edge = jnp.zeros((2, 8 * C, W), BF16)
    gm[0:2] = edge
    gm[8:10] = edge
    edge = jnp.zeros((2, 6 * C, W), BF16)
    low[0:2] = edge
    low[10:12] = edge
    weights = third[...]
    ok_rows = row_ok(8 * C, plane_at - 2, nh)
    for z in range(6):
        y = dot(weights, v3[z : z + 3].reshape(144, W))
        at = depth_at + (z - 1)
        ok = ok_rows & (at >= 0) & (at < nz)
        g = jnp.where(ok, y * slope2[z], 0.0).astype(BF16)
        gm[z + 2] = g
        inner = g[2 * C : 6 * C].astype(F32)
        gm3[z, 0] = from_right(inner).astype(BF16)
        gm3[z, 1] = g[2 * C : 6 * C]
        gm3[z, 2] = from_left(inner).astype(BF16)

    def shifted(ref, slices):
        return jnp.concatenate(
            [
                jnp.concatenate([ref[z, ox, h * C : (h + 1) * C, :] for ox in range(3)], axis=0)
                for z in range(slices)
                for h in range(H)
            ],
            axis=1,
        )

    def windows(ref, slices):
        rows = jnp.concatenate(
            [triple(ref, z, h * C, 3 * C) for z in range(slices) for h in range(H)], axis=1
        )
        return jnp.concatenate([rows, jnp.zeros((96, slices * H * W), BF16)], axis=0)

    terms[...] = jnp.zeros_like(terms)
    term = dot_nt(shifted(gm3, 6), windows(act1, 6))
    terms[0:96] = term[:, 0:128]
    terms[96:192] = term[:, 128:256]
    tail = term[0:24, 256:384]
    for i in range(1, 4):
        tail = tail + pltpu.roll(term[24 * i : 24 * i + 24, 256:384], 32 * i, 1)
    terms[192:216] = tail
    gx_all = jnp.concatenate([gx[i] for i in range(16)], axis=1).astype(BF16)
    term = dot_nt(gx_all, windows(act2, 4))
    for i in range(3):
        terms[216 + 3 * i : 219 + 3 * i] = term[0:3, 128 * i : 128 * i + 128]
    wide = second[...]
    ok_rows = row_ok(6 * C, plane_at - 1, nh)
    for z in range(8):
        y = jnp.concatenate([conv_mid_back(gm, wide, z, h) for h in range(6)], axis=0)
        at = depth_at + (z - 2)
        ok = ok_rows & (at >= 0) & (at < nz)
        g = jnp.where(ok, y * slope1[z], 0.0).astype(BF16)
        low[z + 2] = g
        inner = g[C : 5 * C].astype(F32)
        low3[z, 0] = from_right(inner).astype(BF16)
        low3[z, 1] = g[C : 5 * C]
        low3[z, 2] = from_left(inner).astype(BF16)
    vc_all = jnp.concatenate([vc[i] for i in range(32)], axis=1)
    rows = jnp.concatenate([shifted(low3, 8), jnp.zeros((32, 32 * W), BF16)], axis=0)
    terms[225:234] = dot_nt(vc_all, rows)[0:9]
    chunk = 256 // depth_count
    terms_out[:, 0:chunk, :] = terms[...].reshape(depth_count, chunk, 128).astype(BF16)
    terms_out[:, chunk : chunk + 16, :] = jnp.zeros((depth_count, 16, 128), BF16)
    side[...] = jnp.zeros_like(side)
    last = first[...]
    for z in range(10):
        for h in range(H):
            row = conv_last(low, last, z, h)
            if 3 <= z < 7:
                volume_out[z - 3, h : h + 1, :] = own[h, z - 3 : z - 2, :] + row
            else:
                at = (z % 7) * H + h
                side[z // 7, at : at + 1, :] = row

    @pl.when(pos[0] > 0)
    def _():
        terms_out[pos[0] - 1, chunk : chunk + 16, :] = side[0].astype(BF16)

    @pl.when(pos[0] < depth_count - 1)
    def _():
        terms_out[pos[0] + 1, chunk : chunk + 16, :] = side[1].astype(BF16)


def first_sum_kernel(count, pos, slots, volume, out, volume_out):
    chunk = 256 // count
    total = jnp.sum(slots[:, 0:chunk, :].astype(F32), axis=0, keepdims=True)
    out[...] = jnp.broadcast_to(total, out.shape).astype(BF16)
    before = near_slot(pos, count, slots, -1)[chunk:]
    after = near_slot(pos, count, slots, 1)[chunk:]
    for z in range(Z):
        rows = volume[z]
        if z < 3:
            rows = rows + before[z * H : (z + 1) * H]
        if z > 0:
            rows = rows + after[(z - 1) * H : z * H]
        volume_out[z] = rows


def sum_kernel(sums, out):
    total = jnp.sum(sums[...].astype(F32), axis=0, keepdims=True)
    out[...] = jnp.broadcast_to(total, out.shape).astype(BF16)


def unpack_kernel(scale, sums, in_out, mid_out, out_out):
    full = sums[...].astype(F32).reshape(256, 128) * scale
    quarters = [full] + [pltpu.roll(full, 128 - 32 * j, 1) for j in range(1, 4)]
    last = jnp.concatenate([q[192:216, 0:C] for q in quarters], axis=0)
    for q in range(9):
        for ox in range(3):
            if q < 8:
                start = 96 * (q // 4) + C * ox
                mid_out[q * 3 + ox] = quarters[q % 4][start : start + C, 0:C]
            else:
                mid_out[q * 3 + ox] = last[C * ox : C * ox + C]
        start = 216 + 3 * (q // 4)
        out_out[q * 3 : q * 3 + 3, :] = quarters[q % 4][start : start + 3, 0:C]
        for ox in range(3):
            in_out[q * 3 + ox : q * 3 + ox + 1, :] = quarters[ox][225 + q : 226 + q, 0:C]


def call(kernel, out_shapes, scratch, *args):
    specs = [pl.BlockSpec(memory_space=pltpu.VMEM) for _ in args]
    if args[0].dtype == jnp.int32 and args[0].ndim == 1:
        specs[0] = pl.BlockSpec(memory_space=pltpu.SMEM)
    return pl.pallas_call(
        kernel,
        out_shape=[jax.ShapeDtypeStruct(s, d) for s, d in out_shapes],
        in_specs=specs,
        out_specs=[pl.BlockSpec(memory_space=pltpu.VMEM) for _ in out_shapes],
        scratch_shapes=[pltpu.VMEM(s, d) for s, d in scratch],
        compiler_params=pltpu.CompilerParams(vmem_limit_bytes=40 * 1024 * 1024),
    )(*args)


def swaps(cells, axis):
    count = lax.axis_size(axis)
    first = [(i, i ^ 1) for i in range(count)]
    second = [(i, i + 1 if i % 2 else i - 1) for i in range(1, count - 1)]
    return lax.ppermute(cells, axis, first), lax.ppermute(cells, axis, second)


def scatter_to(cells, axis):
    return lax.all_to_all(cells, axis, 0, 0, tiled=True)


def per_device(volume, cotangent, kernel_in, kernel_mid, kernel_out, measured, angle_ids, ray_bins):
    depths, planes = lax.axis_size(DEPTH), lax.axis_size(PLANE)
    depth_at, plane_at = lax.axis_index(DEPTH), lax.axis_index(PLANE)
    pos = jnp.stack([depth_at, plane_at]).astype(jnp.int32)

    v_first, v_second = swaps(volume, DEPTH)
    first, wide, last, first_back, wide_back, last_back = call(
        weights_kernel,
        [
            ((10 * C, 144), BF16),
            ((3 * C, 9 * C), BF16),
            ((16, 9 * C), BF16),
            ((8 * C, 144), BF16),
            ((3 * C, 9 * C), BF16),
            ((16, 9 * C), BF16),
        ],
        [],
        kernel_in, kernel_mid, kernel_out,
    )
    pack = call(
        pack_kernel,
        [((36, H, W), BF16)],
        [],
        pos, v_first, v_second, volume, cotangent, ray_bins,
    )[0]
    p_first, p_second = swaps(pack, PLANE)

    vc, act1, slope1, act2, slope2, rays = call(
        functools.partial(forward_kernel, depths, planes),
        [
            ((32, 16, W), BF16),
            ((8, 6 * C, W), BF16),
            ((8, 6 * C, W), F32),
            ((6, 6 * C, W), BF16),
            ((6, 8 * C, W), F32),
            ((TILES, 3 * HI, 128), BF16),
        ],
        [
            ((12, 16, W), F32),
            ((12, 48, W), BF16),
            ((32, 16, W), F32),
            ((8, 10 * C, W), BF16),
            ((6, 6 * C, W), BF16),
        ],
        pos, p_first, p_second, pack, first, wide, last, cotangent, ray_bins,
    )
    each = TILES // planes
    gathered = scatter_to(rays.reshape(planes, each * 3 * HI, 128), PLANE)
    tiles = plane_at * each + jnp.arange(each)
    chosen = jnp.stack(
        [
            lax.dynamic_slice(measured, (tiles[t] % Z, angle_ids[tiles[t] // Z], 0), (1, 1, BINS))
            for t in range(each)
        ]
    ).reshape(each, HI, 128)
    spread = call(
        functools.partial(weigh_kernel, planes),
        [((planes, each * HI, 128), BF16)],
        [],
        gathered, chosen,
    )[0]
    weighted = scatter_to(spread, PLANE).reshape(TILES, HI, 128)
    slab, own = call(
        functools.partial(back_kernel, planes),
        [((12, Z, W), BF16), ((H, Z, W), F32)],
        [((12, Z, W), F32)],
        pos, weighted, p_first, p_second, pack, cotangent,
    )
    partial, terms = call(
        functools.partial(backward_kernel, depths, planes),
        [((Z, H, W), F32), ((depths, 256 // depths + 16, 128), BF16)],
        [
            ((8, 16, W), F32),
            ((8, 48, W), BF16),
            ((16, 16, W), F32),
            ((10, 8 * C, W), BF16),
            ((6, 3, 4 * C, W), BF16),
            ((12, 6 * C, W), BF16),
            ((8, 3, 4 * C, W), BF16),
            ((256, 128), F32),
            ((2, 16, W), F32),
        ],
        pos, slab, own, last_back, wide_back, first_back, vc, act1, slope1, act2, slope2,
    )
    sums, grad_volume = call(
        functools.partial(first_sum_kernel, depths),
        [((planes, 256 // depths, 128), BF16), ((Z, H, W), F32)],
        [],
        pos, scatter_to(terms, DEPTH), partial,
    )
    sums = call(
        sum_kernel,
        [((depths, 256 // depths, 128), BF16)],
        [],
        scatter_to(sums, PLANE),
    )[0]
    sums = scatter_to(sums, DEPTH)
    cell_count = Z * depths * H * planes * W
    got_in, got_mid, got_out = call(
        functools.partial(unpack_kernel, float(cell_count) ** (-0.5)),
        [((27, C), F32), ((27, C, C), F32), ((27, C), F32)],
        [],
        sums,
    )
    return (grad_volume, got_in, got_mid, got_out)


def solution(mesh):
    placed = (
        P(DEPTH, PLANE, None),
        P(DEPTH, PLANE, None),
        P(),
        P(),
        P(),
        P(DEPTH, None, None),
        P(),
        P(None, PLANE, None),
    )
    return jax.shard_map(
        per_device,
        mesh=mesh,
        in_specs=placed,
        out_specs=(P(DEPTH, PLANE, None), P(), P(), P()),
        check_vma=False,
    )
```

```python
import functools

import jax
import jax.numpy as jnp
from jax import lax
from jax.experimental import pallas as pl
from jax.experimental.pallas import tpu as pltpu
from jax.sharding import PartitionSpec as P

BINS = 1024
ANG = 8
C = 32
W = 128
Z = 4
H = 4
HI = BINS // 128
TILES = ANG * Z

delta_scale = 6.0

DEPTH = "depth"
PLANE = "plane"
F32 = jnp.float32
BF16 = jnp.bfloat16


def lanes_of(shape):
    return lax.broadcasted_iota(jnp.int32, shape, len(shape) - 1)


def from_left(x):
    lane = lanes_of(x.shape)
    return jnp.where(lane > 0, pltpu.roll(x, 1, x.ndim - 1), 0.0)


def from_right(x):
    lane = lanes_of(x.shape)
    return jnp.where(lane < W - 1, pltpu.roll(x, W - 1, x.ndim - 1), 0.0)


def dot(a, b):
    return jnp.dot(a, b, preferred_element_type=F32)


def dot_nt(a, b):
    return lax.dot_general(a, b, (((1,), (1,)), ((), ())), preferred_element_type=F32)


def row_ok(rows, first, count):
    at = lax.broadcasted_iota(jnp.int32, (rows, W), 0) // C + first
    return (at >= 0) & (at < count)


def banded(base, height, shift):
    rows = [pltpu.roll(base, h + shift, 1) if h + shift else base for h in range(height)]
    return jnp.concatenate(rows, axis=0)[:, :144].astype(BF16)


def base_of(kernel, flip):
    lane = lanes_of((27, 256))
    oz, ox, oy = lane // 48, (lane % 48) // 16, lane % 16
    at = oz * 9 + oy * 3 + ox
    row = lax.broadcasted_iota(jnp.int32, (27, 256), 0)
    take = ((26 - at if flip else at) == row) & (oy < 3) & (lane < 144)
    take = jnp.where(take, 1.0, 0.0).astype(BF16)
    return lax.dot_general(kernel, take, (((0,), (0,)), ((), ())), preferred_element_type=F32)


def tail_of(kernel, flip):
    spot = lax.broadcasted_iota(jnp.int32, (C, 9 * C), 0)
    spread = jnp.where(lanes_of((C, 9 * C)) % C == spot, 1.0, 0.0).astype(BF16)
    wide = dot(kernel, spread)
    row = lax.broadcasted_iota(jnp.int32, (27, 9 * C), 0)
    row = 26 - row if flip else row
    wide = jnp.where(row // 3 == lanes_of((27, 9 * C)) // C, wide, 0.0).astype(BF16)
    lane = lanes_of((16, 27))
    lane = 26 - lane if flip else lane
    pick = lane % 3 == lax.broadcasted_iota(jnp.int32, (16, 27), 0)
    return dot(jnp.where(pick, 1.0, 0.0).astype(BF16), wide).astype(BF16)


def triple(ref, z, start, size):
    return jnp.concatenate([ref[z + oz, start : start + size, :] for oz in range(3)], axis=0)


def three_shifts(ref, flat, count):
    shape = (count, 16, W)
    ref[:, 0:16, :] = from_left(flat).reshape(shape).astype(BF16)
    ref[:, 16:32, :] = flat.reshape(shape).astype(BF16)
    ref[:, 32:48, :] = from_right(flat).reshape(shape).astype(BF16)


def low_match(low_row):
    n = low_row.shape[1]
    at = lax.broadcasted_iota(jnp.int32, (128, n), 0).astype(low_row.dtype)
    return jnp.where(low_row == at, 1.0, 0.0).astype(BF16)


def conv_mid(ref, weights, z, row):
    x = triple(ref, z, row * C, 3 * C)
    y = dot(weights, x)
    return y[C : 2 * C] + from_left(y[0:C]) + from_right(y[2 * C :])


def conv_mid_back(ref, weights, z, row):
    x = jnp.concatenate(
        [
            ref[z + 2 - oz, (row + 2 - oy) * C : (row + 3 - oy) * C, :]
            for oz in range(3)
            for oy in range(3)
        ],
        axis=0,
    )
    y = dot(weights, x)
    return y[C : 2 * C] + from_right(y[0:C]) + from_left(y[2 * C :])


def conv_last(ref, weights, z, row):
    y = dot(weights, triple(ref, z, row * C, 3 * C))
    return y[1:2] + from_left(y[0:1]) + from_right(y[2:3])


def project(field, high, low):
    parts, lows = [], []
    at = lax.broadcasted_iota(jnp.int32, (HI, W), 0).astype(F32)
    for h in range(H):
        match = high[h : h + 1, :] == at
        rows = [jnp.where(match, field[h][r : r + 1, :], 0.0) for r in range(field[h].shape[0])]
        parts.append(jnp.concatenate(rows, axis=0))
        lows.append(low_match(low[h : h + 1, :]))
    part = jnp.concatenate(parts, axis=1)
    low = jnp.concatenate(lows, axis=1)
    head = part.astype(BF16)
    rest = (part - head.astype(F32)).astype(BF16)
    n = part.shape[0]
    both = dot_nt(jnp.concatenate([head, rest], axis=0), low)
    return both[:n] + both[n:]


def local_kernel(cot, bins, first, second, third, pack_out, first_out, wide_out, last_out,
                 first_back, wide_back, last_back):
    head = cot[...].astype(BF16)
    pack_out[0:4] = head
    pack_out[4:8] = (cot[...] - head.astype(F32)).astype(BF16)
    pack_out[8:16] = (bins[...] >> 7).astype(F32).astype(BF16)
    pack_out[16:24] = (bins[...] & 127).astype(F32).astype(BF16)
    first_out[...] = banded(base_of(first[...], False), 10, 0)
    first_back[...] = banded(base_of(third[...], True), 8, 1)
    last_out[...] = tail_of(third[...], False)
    last_back[...] = tail_of(first[...], True)
    for ox in range(3):
        blocks = [second[q * 3 + ox] for q in range(9)]
        wide_out[ox * C : (ox + 1) * C, :] = jnp.concatenate(blocks, axis=1)
        blocks = jnp.concatenate(blocks, axis=0).astype(F32)
        wide_back[ox * C : (ox + 1) * C, :] = blocks.T.astype(BF16)


def near_slot(pos, count, slots, step):
    at = pos[0] + step
    rows = slots[jnp.clip(at, 0, count - 1)].astype(F32)
    return jnp.where((at >= 0) & (at < count), rows, 0.0)


def in_order(at, first, second):
    even = (at & 1) == 0
    return jnp.where(even, second, first), jnp.where(even, first, second)


def pack_kernel(pos, first, second, own, local, out):
    before, after = in_order(pos[0], first[...].astype(F32), second[...].astype(F32))
    out[0:4] = before.astype(BF16)
    out[4:8] = own[...]
    out[8:12] = after.astype(BF16)
    out[12:36] = local[...]


def forward_kernel(depth_count, plane_count, pos, swap_a, swap_b, mid, first, second, third,
                   vc_out, act1_out, slope1_out, act2_out, slope2_out, rays_out,
                   vs, v3, vcs, a1, a2):
    depth_at = pos[0] * Z
    plane_at = pos[1] * H
    nz, nh = depth_count * Z, plane_count * H
    vs[...] = jnp.zeros_like(vs)
    lo, hi = in_order(pos[1], swap_a[0:12].astype(F32), swap_b[0:12].astype(F32))
    vs[:, 0:4, :] = lo
    vs[:, 4:8, :] = mid[0:12].astype(F32)
    vs[:, 8:12, :] = hi
    three_shifts(v3, vs[...].reshape(12 * 16, W), 12)
    vcs[...] = jnp.zeros_like(vcs)
    for z in range(8):
        for h in range(H):
            for oz in range(3):
                vcs[z * H + h, oz * 3 : oz * 3 + 3, :] = vs[z + 1 + oz, h + 3 : h + 6, :]
    vc_out[...] = vcs[...].astype(BF16)
    weights = first[...]
    ok_rows = row_ok(10 * C, plane_at - 3, nh)
    for z in range(8):
        p = dot(weights, v3[z + 1 : z + 4].reshape(144, W))
        sigma = jax.nn.sigmoid(p)
        at = depth_at + (z - 2)
        ok = ok_rows & (at >= 0) & (at < nz)
        act = jnp.where(ok, p * sigma, 0.0).astype(BF16)
        a1[z] = act
        act1_out[z] = act[2 * C : 8 * C]
        slope1_out[z] = (sigma * (1.0 + p * (1.0 - sigma)))[2 * C : 8 * C]
    wide = second[...]
    ok_rows = row_ok(8 * C, plane_at - 2, nh)
    for z in range(6):
        p = jnp.concatenate([conv_mid(a1, wide, z, h) for h in range(8)], axis=0)
        sigma = jax.nn.sigmoid(p)
        at = depth_at + (z - 1)
        ok = ok_rows & (at >= 0) & (at < nz)
        act = jnp.where(ok, p * sigma, 0.0).astype(BF16)
        slope2_out[z] = sigma * (1.0 + p * (1.0 - sigma))
        a2[z] = act[C : 7 * C]
        act2_out[z] = act[C : 7 * C]
    last = third[...]
    local = mid[12:36].astype(F32)
    cot = local[0:4] + local[4:8]
    field = []
    for h in range(H):
        rows = []
        for z in range(Z):
            rows.append(vs[z + 4, h + 4 : h + 5, :] - conv_last(a2, last, z, h))
        for z in range(Z):
            rows.append(cot[z, h : h + 1, :])
        field.append(jnp.concatenate(rows, axis=0))
    for a in range(ANG):
        tile = project(field, local[8 + a], local[16 + a]).reshape(2, Z, HI, 128)
        head = tile[0].astype(BF16).astype(F32)
        rows = jnp.concatenate([head, tile[0] - head, tile[1]], axis=1)
        rays_out[a * Z : (a + 1) * Z] = rows.astype(BF16)


def weigh_kernel(planes, rays, chosen, out):
    each = TILES // planes
    total = jnp.sum(rays[...].astype(F32), axis=0)
    for t in range(each):
        at = t * 3 * HI
        forward = total[at : at + HI] + total[at + HI : at + 2 * HI]
        turned = total[at + 2 * HI : at + 3 * HI]
        ratio = (forward - chosen[t]) / delta_scale
        inner = 1.0 + ratio * ratio
        weighted = turned / (inner * jnp.sqrt(inner))
        weighted = jnp.broadcast_to(weighted[None], (planes, HI, 128))
        out[:, t * HI : (t + 1) * HI, :] = weighted.astype(BF16)


def back_kernel(plane_count, pos, rays, swap_a, swap_b, mid, cot, slab_out, own_out, slab):
    plane_at = pos[1] * H
    nh = plane_count * H
    lo, hi = in_order(pos[1], swap_a[12:36].astype(F32), swap_b[12:36].astype(F32))
    packs = [lo, mid[12:36].astype(F32), hi]
    at = lax.broadcasted_iota(jnp.int32, (HI, W), 0).astype(F32)
    spans = range(1, 11)
    total = [None] * len(spans)
    for a in range(ANG):
        rows = rays[a * Z : (a + 1) * Z].astype(F32).reshape(Z * HI, 128).astype(BF16)
        highs = [packs[h // H][8 + a, h % H : h % H + 1, :] for h in spans]
        lows = [packs[h // H][16 + a, h % H : h % H + 1, :] for h in spans]
        spread = dot(rows, jnp.concatenate([low_match(b) for b in lows], axis=1))
        for i, b in enumerate(highs):
            match = jnp.concatenate([b == at] * Z, axis=0)
            term = jnp.where(match, spread[:, i * W : (i + 1) * W], 0.0)
            total[i] = term if total[i] is None else total[i] + term
    slab[...] = jnp.zeros_like(slab)
    for i, h in enumerate(spans):
        summed = jnp.sum(total[i].reshape(Z, HI, W), axis=1)
        if H <= h < 2 * H:
            rows = cot[:, h - H, :]
        else:
            pack = packs[h // H]
            rows = pack[0:4, h % H, :] + pack[4:8, h % H, :]
        field = rows - (0.25 / ANG) * summed
        row = plane_at + h - H
        slab[h] = jnp.where((row >= 0) & (row < nh), -field, 0.0)
        if H <= h < 2 * H:
            own_out[h - H] = field
    slab_out[...] = slab[...].astype(BF16)


def backward_kernel(depth_count, plane_count, pos, slab, own, first, second, third,
                    vc, act1, slope1, act2, slope2,
                    volume_out, terms_out,
                    gs, v3, gx, gm, gm3, low, low3, terms, side):
    depth_at = pos[0] * Z
    plane_at = pos[1] * H
    nz, nh = depth_count * Z, plane_count * H
    gs[...] = jnp.zeros_like(gs)
    for h in range(12):
        gs[2:6, h, :] = slab[h].astype(F32)
    three_shifts(v3, gs[...].reshape(128, W), 8)
    gx[...] = jnp.zeros_like(gx)
    rows = gs[2:6, 4:8, :].reshape(16, W)
    gx[:, 0, :] = from_right(rows)
    gx[:, 1, :] = rows
    gx[:, 2, :] = from_left(rows)
    edge = jnp.zeros((2, 8 * C, W), BF16)
    gm[0:2] = edge
    gm[8:10] = edge
    edge = jnp.zeros((2, 6 * C, W), BF16)
    low[0:2] = edge
    low[10:12] = edge
    weights = third[...]
    ok_rows = row_ok(8 * C, plane_at - 2, nh)
    for z in range(6):
        y = dot(weights, v3[z : z + 3].reshape(144, W))
        at = depth_at + (z - 1)
        ok = ok_rows & (at >= 0) & (at < nz)
        g = jnp.where(ok, y * slope2[z], 0.0).astype(BF16)
        gm[z + 2] = g
        inner = g[2 * C : 6 * C].astype(F32)
        gm3[z, 0] = from_right(inner).astype(BF16)
        gm3[z, 1] = g[2 * C : 6 * C]
        gm3[z, 2] = from_left(inner).astype(BF16)

    def shifted(ref, slices):
        return jnp.concatenate(
            [
                jnp.concatenate([ref[z, ox, h * C : (h + 1) * C, :] for ox in range(3)], axis=0)
                for z in range(slices)
                for h in range(H)
            ],
            axis=1,
        )

    def windows(ref, slices):
        rows = jnp.concatenate(
            [triple(ref, z, h * C, 3 * C) for z in range(slices) for h in range(H)], axis=1
        )
        return jnp.concatenate([rows, jnp.zeros((96, slices * H * W), BF16)], axis=0)

    terms[...] = jnp.zeros_like(terms)
    term = dot_nt(shifted(gm3, 6), windows(act1, 6))
    terms[0:96] = term[:, 0:128]
    terms[96:192] = term[:, 128:256]
    tail = term[0:24, 256:384]
    for i in range(1, 4):
        tail = tail + pltpu.roll(term[24 * i : 24 * i + 24, 256:384], 32 * i, 1)
    terms[192:216] = tail
    gx_all = jnp.concatenate([gx[i] for i in range(16)], axis=1).astype(BF16)
    term = dot_nt(gx_all, windows(act2, 4))
    for i in range(3):
        terms[216 + 3 * i : 219 + 3 * i] = term[0:3, 128 * i : 128 * i + 128]
    wide = second[...]
    ok_rows = row_ok(6 * C, plane_at - 1, nh)
    for z in range(8):
        y = jnp.concatenate([conv_mid_back(gm, wide, z, h) for h in range(6)], axis=0)
        at = depth_at + (z - 2)
        ok = ok_rows & (at >= 0) & (at < nz)
        g = jnp.where(ok, y * slope1[z], 0.0).astype(BF16)
        low[z + 2] = g
        inner = g[C : 5 * C].astype(F32)
        low3[z, 0] = from_right(inner).astype(BF16)
        low3[z, 1] = g[C : 5 * C]
        low3[z, 2] = from_left(inner).astype(BF16)
    vc_all = jnp.concatenate([vc[i] for i in range(32)], axis=1)
    rows = jnp.concatenate([shifted(low3, 8), jnp.zeros((32, 32 * W), BF16)], axis=0)
    terms[225:234] = dot_nt(vc_all, rows)[0:9]
    chunk = 256 // depth_count
    terms_out[:, 0:chunk, :] = terms[...].reshape(depth_count, chunk, 128).astype(BF16)
    terms_out[:, chunk : chunk + 16, :] = jnp.zeros((depth_count, 16, 128), BF16)
    side[...] = jnp.zeros_like(side)
    last = first[...]
    for z in range(10):
        for h in range(H):
            row = conv_last(low, last, z, h)
            if 3 <= z < 7:
                volume_out[z - 3, h : h + 1, :] = own[h, z - 3 : z - 2, :] + row
            else:
                at = (z % 7) * H + h
                side[z // 7, at : at + 1, :] = row

    @pl.when(pos[0] > 0)
    def _():
        terms_out[pos[0] - 1, chunk : chunk + 16, :] = side[0].astype(BF16)

    @pl.when(pos[0] < depth_count - 1)
    def _():
        terms_out[pos[0] + 1, chunk : chunk + 16, :] = side[1].astype(BF16)


def unpack_kernel(scale, count, pos, sums, slots, volume, volume_out, in_out, mid_out, out_out):
    before = near_slot(pos, count, slots, -1)[256 // count :]
    after = near_slot(pos, count, slots, 1)[256 // count :]
    for z in range(Z):
        rows = volume[z]
        if z < 3:
            rows = rows + before[z * H : (z + 1) * H]
        if z > 0:
            rows = rows + after[(z - 1) * H : z * H]
        volume_out[z] = rows
    full = sums[...].astype(F32).reshape(256, 128) * scale
    quarters = [full] + [pltpu.roll(full, 128 - 32 * j, 1) for j in range(1, 4)]
    last = jnp.concatenate([q[192:216, 0:C] for q in quarters], axis=0)
    for q in range(9):
        for ox in range(3):
            if q < 8:
                start = 96 * (q // 4) + C * ox
                mid_out[q * 3 + ox] = quarters[q % 4][start : start + C, 0:C]
            else:
                mid_out[q * 3 + ox] = last[C * ox : C * ox + C]
        start = 216 + 3 * (q // 4)
        out_out[q * 3 : q * 3 + 3, :] = quarters[q % 4][start : start + 3, 0:C]
        for ox in range(3):
            in_out[q * 3 + ox : q * 3 + ox + 1, :] = quarters[ox][225 + q : 226 + q, 0:C]


def call(kernel, out_shapes, scratch, *args):
    specs = [pl.BlockSpec(memory_space=pltpu.VMEM) for _ in args]
    if args[0].dtype == jnp.int32 and args[0].ndim == 1:
        specs[0] = pl.BlockSpec(memory_space=pltpu.SMEM)
    return pl.pallas_call(
        kernel,
        out_shape=[jax.ShapeDtypeStruct(s, d) for s, d in out_shapes],
        in_specs=specs,
        out_specs=[pl.BlockSpec(memory_space=pltpu.VMEM) for _ in out_shapes],
        scratch_shapes=[pltpu.VMEM(s, d) for s, d in scratch],
        compiler_params=pltpu.CompilerParams(vmem_limit_bytes=40 * 1024 * 1024),
    )(*args)


def swaps(cells, axis):
    count = lax.axis_size(axis)
    first = [(i, i ^ 1) for i in range(count)]
    second = [(i, i + 1 if i % 2 else i - 1) for i in range(1, count - 1)]
    return lax.ppermute(cells, axis, first), lax.ppermute(cells, axis, second)


def scatter_to(cells, axis):
    return lax.all_to_all(cells, axis, 0, 0, tiled=True)


def per_device(volume, cotangent, kernel_in, kernel_mid, kernel_out, measured, angle_ids, ray_bins):
    depths, planes = lax.axis_size(DEPTH), lax.axis_size(PLANE)
    depth_at, plane_at = lax.axis_index(DEPTH), lax.axis_index(PLANE)
    pos = jnp.stack([depth_at, plane_at]).astype(jnp.int32)

    v_first, v_second = swaps(volume, DEPTH)
    local, first, wide, last, first_back, wide_back, last_back = call(
        local_kernel,
        [
            ((24, H, W), BF16),
            ((10 * C, 144), BF16),
            ((3 * C, 9 * C), BF16),
            ((16, 9 * C), BF16),
            ((8 * C, 144), BF16),
            ((3 * C, 9 * C), BF16),
            ((16, 9 * C), BF16),
        ],
        [],
        cotangent, ray_bins, kernel_in, kernel_mid, kernel_out,
    )
    pack = call(pack_kernel, [((36, H, W), BF16)], [], pos, v_first, v_second, volume, local)[0]
    p_first, p_second = swaps(pack, PLANE)

    vc, act1, slope1, act2, slope2, rays = call(
        functools.partial(forward_kernel, depths, planes),
        [
            ((32, 16, W), BF16),
            ((8, 6 * C, W), BF16),
            ((8, 6 * C, W), F32),
            ((6, 6 * C, W), BF16),
            ((6, 8 * C, W), F32),
            ((TILES, 3 * HI, 128), BF16),
        ],
        [
            ((12, 16, W), F32),
            ((12, 48, W), BF16),
            ((32, 16, W), F32),
            ((8, 10 * C, W), BF16),
            ((6, 6 * C, W), BF16),
        ],
        pos, p_first, p_second, pack, first, wide, last,
    )
    each = TILES // planes
    gathered = scatter_to(rays.reshape(planes, each * 3 * HI, 128), PLANE)
    tiles = plane_at * each + jnp.arange(each)
    chosen = jnp.stack(
        [
            lax.dynamic_slice(measured, (tiles[t] % Z, angle_ids[tiles[t] // Z], 0), (1, 1, BINS))
            for t in range(each)
        ]
    ).reshape(each, HI, 128)
    spread = call(
        functools.partial(weigh_kernel, planes),
        [((planes, each * HI, 128), BF16)],
        [],
        gathered, chosen,
    )[0]
    weighted = scatter_to(spread, PLANE).reshape(TILES, HI, 128)
    slab, own = call(
        functools.partial(back_kernel, planes),
        [((12, Z, W), BF16), ((H, Z, W), F32)],
        [((12, Z, W), F32)],
        pos, weighted, p_first, p_second, pack, cotangent,
    )
    partial, terms = call(
        functools.partial(backward_kernel, depths, planes),
        [((Z, H, W), F32), ((depths, 256 // depths + 16, 128), BF16)],
        [
            ((8, 16, W), F32),
            ((8, 48, W), BF16),
            ((16, 16, W), F32),
            ((10, 8 * C, W), BF16),
            ((6, 3, 4 * C, W), BF16),
            ((12, 6 * C, W), BF16),
            ((8, 3, 4 * C, W), BF16),
            ((256, 128), F32),
            ((2, 16, W), F32),
        ],
        pos, slab, own, last_back, wide_back, first_back, vc, act1, slope1, act2, slope2,
    )
    chunk = 256 // depths

    def spread_sum(cells, count):
        total = jnp.sum(cells[:, :chunk].astype(F32), axis=0, keepdims=True).astype(BF16)
        return jnp.broadcast_to(total, (count,) + total.shape[1:])

    slots = scatter_to(terms, DEPTH)
    sums = scatter_to(spread_sum(slots, planes), PLANE)
    sums = scatter_to(spread_sum(sums, depths), DEPTH)
    cell_count = Z * depths * H * planes * W
    grad_volume, got_in, got_mid, got_out = call(
        functools.partial(unpack_kernel, float(cell_count) ** (-0.5), depths),
        [((Z, H, W), F32), ((27, C), F32), ((27, C, C), F32), ((27, C), F32)],
        [],
        pos, sums, slots, partial,
    )
    return (grad_volume, got_in, got_mid, got_out)


def solution(mesh):
    placed = (
        P(DEPTH, PLANE, None),
        P(DEPTH, PLANE, None),
        P(),
        P(),
        P(),
        P(DEPTH, None, None),
        P(),
        P(None, PLANE, None),
    )
    return jax.shard_map(
        per_device,
        mesh=mesh,
        in_specs=placed,
        out_specs=(P(DEPTH, PLANE, None), P(), P(), P()),
        check_vma=False,
    )
```

```python
import functools

import jax
import jax.numpy as jnp
from jax import lax
from jax.experimental import pallas as pl
from jax.experimental.pallas import tpu as pltpu
from jax.sharding import PartitionSpec as P

BINS = 1024
ANG = 8
C = 32
W = 128
Z = 4
H = 4
HI = BINS // 128
TILES = ANG * Z

delta_scale = 6.0

DEPTH = "depth"
PLANE = "plane"
F32 = jnp.float32
BF16 = jnp.bfloat16


def lanes_of(shape):
    return lax.broadcasted_iota(jnp.int32, shape, len(shape) - 1)


def from_left(x):
    lane = lanes_of(x.shape)
    return jnp.where(lane > 0, pltpu.roll(x, 1, x.ndim - 1), 0.0)


def from_right(x):
    lane = lanes_of(x.shape)
    return jnp.where(lane < W - 1, pltpu.roll(x, W - 1, x.ndim - 1), 0.0)


def dot(a, b):
    return jnp.dot(a, b, preferred_element_type=F32)


def dot_nt(a, b):
    return lax.dot_general(a, b, (((1,), (1,)), ((), ())), preferred_element_type=F32)


def row_ok(rows, first, count):
    at = lax.broadcasted_iota(jnp.int32, (rows, W), 0) // C + first
    return (at >= 0) & (at < count)


def banded(base, height, shift):
    rows = [pltpu.roll(base, h + shift, 1) if h + shift else base for h in range(height)]
    return jnp.concatenate(rows, axis=0)[:, :144].astype(BF16)


def base_of(kernel, flip):
    lane = lanes_of((27, 256))
    oz, ox, oy = lane // 48, (lane % 48) // 16, lane % 16
    at = oz * 9 + oy * 3 + ox
    row = lax.broadcasted_iota(jnp.int32, (27, 256), 0)
    take = ((26 - at if flip else at) == row) & (oy < 3) & (lane < 144)
    take = jnp.where(take, 1.0, 0.0).astype(BF16)
    return lax.dot_general(kernel, take, (((0,), (0,)), ((), ())), preferred_element_type=F32)


def tail_of(kernel, flip):
    spot = lax.broadcasted_iota(jnp.int32, (C, 9 * C), 0)
    spread = jnp.where(lanes_of((C, 9 * C)) % C == spot, 1.0, 0.0).astype(BF16)
    wide = dot(kernel, spread)
    row = lax.broadcasted_iota(jnp.int32, (27, 9 * C), 0)
    row = 26 - row if flip else row
    wide = jnp.where(row // 3 == lanes_of((27, 9 * C)) // C, wide, 0.0).astype(BF16)
    lane = lanes_of((16, 27))
    lane = 26 - lane if flip else lane
    pick = lane % 3 == lax.broadcasted_iota(jnp.int32, (16, 27), 0)
    return banded_tail(dot(jnp.where(pick, 1.0, 0.0).astype(BF16), wide))


def triple(ref, z, start, size):
    return jnp.concatenate([ref[z + oz, start : start + size, :] for oz in range(3)], axis=0)


def three_shifts(ref, flat, count):
    shape = (count, 16, W)
    ref[:, 0:16, :] = from_left(flat).reshape(shape).astype(BF16)
    ref[:, 16:32, :] = flat.reshape(shape).astype(BF16)
    ref[:, 32:48, :] = from_right(flat).reshape(shape).astype(BF16)


def low_match(low_row):
    n = low_row.shape[1]
    at = lax.broadcasted_iota(jnp.int32, (128, n), 0).astype(low_row.dtype)
    return jnp.where(low_row == at, 1.0, 0.0).astype(BF16)


def join(y):
    n = y.shape[0] // 3
    return y[n : 2 * n] + from_left(y[0:n]) + from_right(y[2 * n :])


def pairs(weights, windows):
    out = []
    for i in range(0, len(windows), 2):
        y = dot(weights, jnp.concatenate(windows[i : i + 2], axis=1))
        out += [y[:, :W], y[:, W:]]
    return out


def conv_mid(ref, weights, z, count):
    ys = pairs(weights, [triple(ref, z, h * C, 3 * C) for h in range(count)])
    return jnp.concatenate([join(y) for y in ys], axis=0)


def conv_mid_back(ref, weights, z, count):
    windows = [
        jnp.concatenate(
            [
                ref[z + 2 - oz, (row + 2 - oy) * C : (row + 3 - oy) * C, :]
                for oz in range(3)
                for oy in range(3)
            ],
            axis=0,
        )
        for row in range(count)
    ]
    ys = pairs(weights, windows)
    return jnp.concatenate(
        [y[C : 2 * C] + from_right(y[0:C]) + from_left(y[2 * C :]) for y in ys], axis=0
    )


def conv_last(ref, weights, slices):
    ys = pairs(weights, [triple(ref, z, 0, 6 * C) for z in range(slices)])
    return [join(y) for y in ys]


def banded_tail(tail):
    moved = []
    for h in range(H):
        parts = []
        for oz in range(3):
            if h:
                parts.append(jnp.zeros((16, C * h), F32))
            parts.append(tail[:, 96 * oz : 96 * oz + 96])
            if h < 3:
                parts.append(jnp.zeros((16, 96 - C * h), F32))
        moved.append(jnp.concatenate(parts, axis=1))
    rows = []
    for ox in range(3):
        rows += [m[ox : ox + 1] for m in moved] + [jnp.zeros((8 - H, 18 * C), F32)]
    return jnp.concatenate(rows, axis=0).astype(BF16)


def project(field, high, low):
    parts = []
    at = lax.broadcasted_iota(jnp.int32, (HI, W), 0).astype(F32)
    for h in range(H):
        match = high[h : h + 1, :] == at
        rows = [jnp.where(match, field[h][r : r + 1, :], 0.0) for r in range(field[h].shape[0])]
        parts.append(jnp.concatenate(rows, axis=0))
    part = jnp.concatenate(parts, axis=1)
    head = part.astype(BF16)
    rest = (part - head.astype(F32)).astype(BF16)
    n = part.shape[0]
    both = dot_nt(jnp.concatenate([head, rest], axis=0), low)
    return both[:n] + both[n:]


def local_kernel(cot, bins, first, second, third, pack_out, lows_out, first_out, wide_out, last_out,
                 first_back, wide_back, last_back):
    head = cot[...].astype(BF16)
    pack_out[0:4] = head
    pack_out[4:8] = (cot[...] - head.astype(F32)).astype(BF16)
    pack_out[8:16] = (bins[...] >> 7).astype(F32).astype(BF16)
    pack_out[16:24] = (bins[...] & 127).astype(F32).astype(BF16)
    for a in range(ANG):
        for h in range(H):
            lows_out[a, :, h * W : (h + 1) * W] = low_match(bins[a, h : h + 1, :] & 127)
    first_out[...] = banded(base_of(first[...], False), 10, 0)
    first_back[...] = banded(base_of(third[...], True), 8, 1)
    last_out[...] = tail_of(third[...], False)
    last_back[...] = tail_of(first[...], True)
    for ox in range(3):
        blocks = [second[q * 3 + ox] for q in range(9)]
        wide_out[ox * C : (ox + 1) * C, :] = jnp.concatenate(blocks, axis=1)
        blocks = jnp.concatenate(blocks, axis=0).astype(F32)
        wide_back[ox * C : (ox + 1) * C, :] = blocks.T.astype(BF16)


def near_slot(pos, count, slots, step):
    at = pos[0] + step
    rows = slots[jnp.clip(at, 0, count - 1)].astype(F32)
    return jnp.where((at >= 0) & (at < count), rows, 0.0)


def in_order(at, first, second):
    even = (at & 1) == 0
    return jnp.where(even, second, first), jnp.where(even, first, second)


def pack_kernel(pos, first, second, own, local, out):
    before, after = in_order(pos[0], first[...].astype(F32), second[...].astype(F32))
    out[0:4] = before.astype(BF16)
    out[4:8] = own[...]
    out[8:12] = after.astype(BF16)
    out[12:36] = local[...]


def forward_kernel(depth_count, plane_count, pos, swap_a, swap_b, mid, lows, first, second, third,
                   vc_out, act1_out, slope1_out, act2_out, slope2_out, rays_out,
                   vs, v3, vcs, a1, a2):
    depth_at = pos[0] * Z
    plane_at = pos[1] * H
    nz, nh = depth_count * Z, plane_count * H
    vs[...] = jnp.zeros_like(vs)
    lo, hi = in_order(pos[1], swap_a[0:12].astype(F32), swap_b[0:12].astype(F32))
    vs[:, 0:4, :] = lo
    vs[:, 4:8, :] = mid[0:12].astype(F32)
    vs[:, 8:12, :] = hi
    three_shifts(v3, vs[...].reshape(12 * 16, W), 12)
    vcs[...] = jnp.zeros_like(vcs)
    for z in range(8):
        for h in range(H):
            for oz in range(3):
                vcs[z * H + h, oz * 3 : oz * 3 + 3, :] = vs[z + 1 + oz, h + 3 : h + 6, :]
    vc_out[...] = vcs[...].astype(BF16)
    weights = first[...]
    ok_rows = row_ok(10 * C, plane_at - 3, nh)
    ps = pairs(weights, [v3[z + 1 : z + 4].reshape(144, W) for z in range(8)])
    for z in range(8):
        p = ps[z]
        sigma = jax.nn.sigmoid(p)
        at = depth_at + (z - 2)
        ok = ok_rows & (at >= 0) & (at < nz)
        act = jnp.where(ok, p * sigma, 0.0).astype(BF16)
        a1[z] = act
        act1_out[z] = act[2 * C : 8 * C]
        slope1_out[z] = (sigma * (1.0 + p * (1.0 - sigma)))[2 * C : 8 * C]
    wide = second[...]
    ok_rows = row_ok(8 * C, plane_at - 2, nh)
    for z in range(6):
        p = conv_mid(a1, wide, z, 8)
        sigma = jax.nn.sigmoid(p)
        at = depth_at + (z - 1)
        ok = ok_rows & (at >= 0) & (at < nz)
        act = jnp.where(ok, p * sigma, 0.0).astype(BF16)
        slope2_out[z] = sigma * (1.0 + p * (1.0 - sigma))
        a2[z] = act[C : 7 * C]
        act2_out[z] = act[C : 7 * C]
    last = third[...]
    local = mid[12:36].astype(F32)
    cot = local[0:4] + local[4:8]
    field = []
    dens = [vs[z + 4, 4:8, :] - y[0:H] for z, y in enumerate(conv_last(a2, last, Z))]
    for h in range(H):
        rows = [den[h : h + 1] for den in dens]
        for z in range(Z):
            rows.append(cot[z, h : h + 1, :])
        field.append(jnp.concatenate(rows, axis=0))
    for a in range(ANG):
        tile = project(field, local[8 + a], lows[a]).reshape(2, Z, HI, 128)
        head = tile[0].astype(BF16).astype(F32)
        rows = jnp.concatenate([head, tile[0] - head, tile[1]], axis=1)
        rays_out[a * Z : (a + 1) * Z] = rows.astype(BF16)


def weigh_kernel(planes, rays, chosen, out):
    each = TILES // planes
    total = jnp.sum(rays[...].astype(F32), axis=0)
    for t in range(each):
        at = t * 3 * HI
        forward = total[at : at + HI] + total[at + HI : at + 2 * HI]
        turned = total[at + 2 * HI : at + 3 * HI]
        ratio = (forward - chosen[t]) / delta_scale
        inner = 1.0 + ratio * ratio
        weighted = turned / (inner * jnp.sqrt(inner))
        weighted = jnp.broadcast_to(weighted[None], (planes, HI, 128))
        out[:, t * HI : (t + 1) * HI, :] = weighted.astype(BF16)


def back_kernel(plane_count, pos, rays, swap_a, swap_b, mid, cot, slab_out, own_out, slab):
    plane_at = pos[1] * H
    nh = plane_count * H
    lo, hi = in_order(pos[1], swap_a[12:36].astype(F32), swap_b[12:36].astype(F32))
    packs = [lo, mid[12:36].astype(F32), hi]
    at = lax.broadcasted_iota(jnp.int32, (HI, W), 0).astype(F32)
    spans = range(1, 11)
    total = [None] * len(spans)
    for a in range(ANG):
        rows = rays[a * Z : (a + 1) * Z].astype(F32).reshape(Z * HI, 128).astype(BF16)
        highs = [packs[h // H][8 + a, h % H : h % H + 1, :] for h in spans]
        lows = [packs[h // H][16 + a, h % H : h % H + 1, :] for h in spans]
        spread = dot(rows, jnp.concatenate([low_match(b) for b in lows], axis=1))
        for i, b in enumerate(highs):
            match = jnp.concatenate([b == at] * Z, axis=0)
            term = jnp.where(match, spread[:, i * W : (i + 1) * W], 0.0)
            total[i] = term if total[i] is None else total[i] + term
    slab[...] = jnp.zeros_like(slab)
    for i, h in enumerate(spans):
        summed = jnp.sum(total[i].reshape(Z, HI, W), axis=1)
        if H <= h < 2 * H:
            rows = cot[:, h - H, :]
        else:
            pack = packs[h // H]
            rows = pack[0:4, h % H, :] + pack[4:8, h % H, :]
        field = rows - (0.25 / ANG) * summed
        row = plane_at + h - H
        slab[h] = jnp.where((row >= 0) & (row < nh), -field, 0.0)
        if H <= h < 2 * H:
            own_out[h - H] = field
    slab_out[...] = slab[...].astype(BF16)


def backward_kernel(depth_count, plane_count, pos, slab, own, first, second, third,
                    vc, act1, slope1, act2, slope2,
                    volume_out, terms_out,
                    gs, v3, gx, gm, gm3, low, low3, terms, side):
    depth_at = pos[0] * Z
    plane_at = pos[1] * H
    nz, nh = depth_count * Z, plane_count * H
    gs[...] = jnp.zeros_like(gs)
    for h in range(12):
        gs[2:6, h, :] = slab[h].astype(F32)
    three_shifts(v3, gs[...].reshape(128, W), 8)
    gx[...] = jnp.zeros_like(gx)
    rows = gs[2:6, 4:8, :].reshape(16, W)
    gx[:, 0, :] = from_right(rows)
    gx[:, 1, :] = rows
    gx[:, 2, :] = from_left(rows)
    edge = jnp.zeros((2, 8 * C, W), BF16)
    gm[0:2] = edge
    gm[8:10] = edge
    edge = jnp.zeros((2, 6 * C, W), BF16)
    low[0:2] = edge
    low[10:12] = edge
    weights = third[...]
    ok_rows = row_ok(8 * C, plane_at - 2, nh)
    ys = pairs(weights, [v3[z : z + 3].reshape(144, W) for z in range(6)])
    for z in range(6):
        y = ys[z]
        at = depth_at + (z - 1)
        ok = ok_rows & (at >= 0) & (at < nz)
        g = jnp.where(ok, y * slope2[z], 0.0).astype(BF16)
        gm[z + 2] = g
        inner = g[2 * C : 6 * C].astype(F32)
        gm3[z, 0] = from_right(inner).astype(BF16)
        gm3[z, 1] = g[2 * C : 6 * C]
        gm3[z, 2] = from_left(inner).astype(BF16)

    def shifted(ref, slices):
        return jnp.concatenate(
            [
                jnp.concatenate([ref[z, ox, h * C : (h + 1) * C, :] for ox in range(3)], axis=0)
                for z in range(slices)
                for h in range(H)
            ],
            axis=1,
        )

    def windows(ref, slices):
        rows = jnp.concatenate(
            [triple(ref, z, h * C, 3 * C) for z in range(slices) for h in range(H)], axis=1
        )
        return jnp.concatenate([rows, jnp.zeros((96, slices * H * W), BF16)], axis=0)

    terms[...] = jnp.zeros_like(terms)
    term = dot_nt(shifted(gm3, 6), windows(act1, 6))
    terms[0:96] = term[:, 0:128]
    terms[96:192] = term[:, 128:256]
    tail = term[0:24, 256:384]
    for i in range(1, 4):
        tail = tail + pltpu.roll(term[24 * i : 24 * i + 24, 256:384], 32 * i, 1)
    terms[192:216] = tail
    gx_all = jnp.concatenate([gx[i] for i in range(16)], axis=1).astype(BF16)
    term = dot_nt(gx_all, windows(act2, 4))
    for i in range(3):
        terms[216 + 3 * i : 219 + 3 * i] = term[0:3, 128 * i : 128 * i + 128]
    wide = second[...]
    ok_rows = row_ok(6 * C, plane_at - 1, nh)
    for z in range(8):
        y = conv_mid_back(gm, wide, z, 6)
        at = depth_at + (z - 2)
        ok = ok_rows & (at >= 0) & (at < nz)
        g = jnp.where(ok, y * slope1[z], 0.0).astype(BF16)
        low[z + 2] = g
        inner = g[C : 5 * C].astype(F32)
        low3[z, 0] = from_right(inner).astype(BF16)
        low3[z, 1] = g[C : 5 * C]
        low3[z, 2] = from_left(inner).astype(BF16)
    vc_all = jnp.concatenate([vc[i] for i in range(32)], axis=1)
    rows = jnp.concatenate([shifted(low3, 8), jnp.zeros((32, 32 * W), BF16)], axis=0)
    terms[225:234] = dot_nt(vc_all, rows)[0:9]
    chunk = 256 // depth_count
    terms_out[:, 0:chunk, :] = terms[...].reshape(depth_count, chunk, 128).astype(BF16)
    terms_out[:, chunk : chunk + 16, :] = jnp.zeros((depth_count, 16, 128), BF16)
    side[...] = jnp.zeros_like(side)
    last = first[...]
    for z, y in enumerate(conv_last(low, last, 10)):
        if 3 <= z < 7:
            volume_out[z - 3] = own[:, z - 3, :] + y[0:H]
        else:
            at = (z % 7) * H
            side[z // 7, at : at + H, :] = y[0:H]

    @pl.when(pos[0] > 0)
    def _():
        terms_out[pos[0] - 1, chunk : chunk + 16, :] = side[0].astype(BF16)

    @pl.when(pos[0] < depth_count - 1)
    def _():
        terms_out[pos[0] + 1, chunk : chunk + 16, :] = side[1].astype(BF16)


def unpack_kernel(scale, count, pos, sums, slots, volume, volume_out, in_out, mid_out, out_out):
    before = near_slot(pos, count, slots, -1)[256 // count :]
    after = near_slot(pos, count, slots, 1)[256 // count :]
    for z in range(Z):
        rows = volume[z]
        if z < 3:
            rows = rows + before[z * H : (z + 1) * H]
        if z > 0:
            rows = rows + after[(z - 1) * H : z * H]
        volume_out[z] = rows
    full = sums[...].astype(F32).reshape(256, 128) * scale
    quarters = [full] + [pltpu.roll(full, 128 - 32 * j, 1) for j in range(1, 4)]
    last = jnp.concatenate([q[192:216, 0:C] for q in quarters], axis=0)
    for q in range(9):
        for ox in range(3):
            if q < 8:
                start = 96 * (q // 4) + C * ox
                mid_out[q * 3 + ox] = quarters[q % 4][start : start + C, 0:C]
            else:
                mid_out[q * 3 + ox] = last[C * ox : C * ox + C]
        start = 216 + 3 * (q // 4)
        out_out[q * 3 : q * 3 + 3, :] = quarters[q % 4][start : start + 3, 0:C]
        for ox in range(3):
            in_out[q * 3 + ox : q * 3 + ox + 1, :] = quarters[ox][225 + q : 226 + q, 0:C]


def call(kernel, out_shapes, scratch, *args):
    specs = [pl.BlockSpec(memory_space=pltpu.VMEM) for _ in args]
    if args[0].dtype == jnp.int32 and args[0].ndim == 1:
        specs[0] = pl.BlockSpec(memory_space=pltpu.SMEM)
    return pl.pallas_call(
        kernel,
        out_shape=[jax.ShapeDtypeStruct(s, d) for s, d in out_shapes],
        in_specs=specs,
        out_specs=[pl.BlockSpec(memory_space=pltpu.VMEM) for _ in out_shapes],
        scratch_shapes=[pltpu.VMEM(s, d) for s, d in scratch],
        compiler_params=pltpu.CompilerParams(vmem_limit_bytes=40 * 1024 * 1024),
    )(*args)


def swaps(cells, axis):
    count = lax.axis_size(axis)
    first = [(i, i ^ 1) for i in range(count)]
    second = [(i, i + 1 if i % 2 else i - 1) for i in range(1, count - 1)]
    return lax.ppermute(cells, axis, first), lax.ppermute(cells, axis, second)


def scatter_to(cells, axis):
    return lax.all_to_all(cells, axis, 0, 0, tiled=True)


def per_device(volume, cotangent, kernel_in, kernel_mid, kernel_out, measured, angle_ids, ray_bins):
    depths, planes = lax.axis_size(DEPTH), lax.axis_size(PLANE)
    depth_at, plane_at = lax.axis_index(DEPTH), lax.axis_index(PLANE)
    pos = jnp.stack([depth_at, plane_at]).astype(jnp.int32)

    v_first, v_second = swaps(volume, DEPTH)
    local, lows, first, wide, last, first_back, wide_back, last_back = call(
        local_kernel,
        [
            ((24, H, W), BF16),
            ((ANG, 128, H * W), BF16),
            ((10 * C, 144), BF16),
            ((3 * C, 9 * C), BF16),
            ((24, 18 * C), BF16),
            ((8 * C, 144), BF16),
            ((3 * C, 9 * C), BF16),
            ((24, 18 * C), BF16),
        ],
        [],
        cotangent, ray_bins, kernel_in, kernel_mid, kernel_out,
    )
    pack = call(pack_kernel, [((36, H, W), BF16)], [], pos, v_first, v_second, volume, local)[0]
    p_first, p_second = swaps(pack, PLANE)

    vc, act1, slope1, act2, slope2, rays = call(
        functools.partial(forward_kernel, depths, planes),
        [
            ((32, 16, W), BF16),
            ((8, 6 * C, W), BF16),
            ((8, 6 * C, W), F32),
            ((6, 6 * C, W), BF16),
            ((6, 8 * C, W), F32),
            ((TILES, 3 * HI, 128), BF16),
        ],
        [
            ((12, 16, W), F32),
            ((12, 48, W), BF16),
            ((32, 16, W), F32),
            ((8, 10 * C, W), BF16),
            ((6, 6 * C, W), BF16),
        ],
        pos, p_first, p_second, pack, lows, first, wide, last,
    )
    each = TILES // planes
    gathered = scatter_to(rays.reshape(planes, each * 3 * HI, 128), PLANE)
    tiles = plane_at * each + jnp.arange(each)
    chosen = jnp.stack(
        [
            lax.dynamic_slice(measured, (tiles[t] % Z, angle_ids[tiles[t] // Z], 0), (1, 1, BINS))
            for t in range(each)
        ]
    ).reshape(each, HI, 128)
    spread = call(
        functools.partial(weigh_kernel, planes),
        [((planes, each * HI, 128), BF16)],
        [],
        gathered, chosen,
    )[0]
    weighted = scatter_to(spread, PLANE).reshape(TILES, HI, 128)
    slab, own = call(
        functools.partial(back_kernel, planes),
        [((12, Z, W), BF16), ((H, Z, W), F32)],
        [((12, Z, W), F32)],
        pos, weighted, p_first, p_second, pack, cotangent,
    )
    partial, terms = call(
        functools.partial(backward_kernel, depths, planes),
        [((Z, H, W), F32), ((depths, 256 // depths + 16, 128), BF16)],
        [
            ((8, 16, W), F32),
            ((8, 48, W), BF16),
            ((16, 16, W), F32),
            ((10, 8 * C, W), BF16),
            ((6, 3, 4 * C, W), BF16),
            ((12, 6 * C, W), BF16),
            ((8, 3, 4 * C, W), BF16),
            ((256, 128), F32),
            ((2, 16, W), F32),
        ],
        pos, slab, own, last_back, wide_back, first_back, vc, act1, slope1, act2, slope2,
    )
    chunk = 256 // depths

    def spread_sum(cells, count):
        total = jnp.sum(cells[:, :chunk].astype(F32), axis=0, keepdims=True).astype(BF16)
        return jnp.broadcast_to(total, (count,) + total.shape[1:])

    slots = scatter_to(terms, DEPTH)
    sums = scatter_to(spread_sum(slots, planes), PLANE)
    sums = scatter_to(spread_sum(sums, depths), DEPTH)
    cell_count = Z * depths * H * planes * W
    grad_volume, got_in, got_mid, got_out = call(
        functools.partial(unpack_kernel, float(cell_count) ** (-0.5), depths),
        [((Z, H, W), F32), ((27, C), F32), ((27, C, C), F32), ((27, C), F32)],
        [],
        pos, sums, slots, partial,
    )
    return (grad_volume, got_in, got_mid, got_out)


def solution(mesh):
    placed = (
        P(DEPTH, PLANE, None),
        P(DEPTH, PLANE, None),
        P(),
        P(),
        P(),
        P(DEPTH, None, None),
        P(),
        P(None, PLANE, None),
    )
    return jax.shard_map(
        per_device,
        mesh=mesh,
        in_specs=placed,
        out_specs=(P(DEPTH, PLANE, None), P(), P(), P()),
        check_vma=False,
    )
```

```python
import functools

import jax
import jax.numpy as jnp
from jax import lax
from jax.experimental import pallas as pl
from jax.experimental.pallas import tpu as pltpu
from jax.sharding import PartitionSpec as P

BINS = 1024
ANG = 8
C = 32
W = 128
Z = 4
H = 4
HI = BINS // 128
TILES = ANG * Z

delta_scale = 6.0

DEPTH = "depth"
PLANE = "plane"
F32 = jnp.float32
BF16 = jnp.bfloat16


def lanes_of(shape):
    return lax.broadcasted_iota(jnp.int32, shape, len(shape) - 1)


def from_left(x):
    lane = lanes_of(x.shape)
    return jnp.where(lane > 0, pltpu.roll(x, 1, x.ndim - 1), 0.0)


def from_right(x):
    lane = lanes_of(x.shape)
    return jnp.where(lane < W - 1, pltpu.roll(x, W - 1, x.ndim - 1), 0.0)


def dot(a, b):
    return jnp.dot(a, b, preferred_element_type=F32)


def dot_nt(a, b):
    return lax.dot_general(a, b, (((1,), (1,)), ((), ())), preferred_element_type=F32)


def row_ok(rows, first, count):
    at = lax.broadcasted_iota(jnp.int32, (rows, W), 0) // C + first
    return (at >= 0) & (at < count)


def banded(base, height, shift):
    rows = [pltpu.roll(base, h + shift, 1) if h + shift else base for h in range(height)]
    return jnp.concatenate(rows, axis=0)[:, :144].astype(BF16)


def base_of(kernel, flip):
    lane = lanes_of((27, 256))
    oz, ox, oy = lane // 48, (lane % 48) // 16, lane % 16
    at = oz * 9 + oy * 3 + ox
    row = lax.broadcasted_iota(jnp.int32, (27, 256), 0)
    take = ((26 - at if flip else at) == row) & (oy < 3) & (lane < 144)
    take = jnp.where(take, 1.0, 0.0).astype(BF16)
    return lax.dot_general(kernel, take, (((0,), (0,)), ((), ())), preferred_element_type=F32)


def tail_of(kernel, flip):
    spot = lax.broadcasted_iota(jnp.int32, (C, 9 * C), 0)
    spread = jnp.where(lanes_of((C, 9 * C)) % C == spot, 1.0, 0.0).astype(BF16)
    wide = dot(kernel, spread)
    row = lax.broadcasted_iota(jnp.int32, (27, 9 * C), 0)
    row = 26 - row if flip else row
    wide = jnp.where(row // 3 == lanes_of((27, 9 * C)) // C, wide, 0.0).astype(BF16)
    lane = lanes_of((16, 27))
    lane = 26 - lane if flip else lane
    pick = lane % 3 == lax.broadcasted_iota(jnp.int32, (16, 27), 0)
    return banded_tail(dot(jnp.where(pick, 1.0, 0.0).astype(BF16), wide))


def triple(ref, z, start, size):
    return jnp.concatenate([ref[z + oz, start : start + size, :] for oz in range(3)], axis=0)


def three_shifts(ref, flat, count):
    shape = (count, 16, W)
    ref[:, 0:16, :] = from_left(flat).reshape(shape).astype(BF16)
    ref[:, 16:32, :] = flat.reshape(shape).astype(BF16)
    ref[:, 32:48, :] = from_right(flat).reshape(shape).astype(BF16)


def low_match(low_row):
    n = low_row.shape[1]
    at = lax.broadcasted_iota(jnp.int32, (128, n), 0).astype(low_row.dtype)
    return jnp.where(low_row == at, 1.0, 0.0).astype(BF16)


def join(y):
    n = y.shape[0] // 3
    return y[n : 2 * n] + from_left(y[0:n]) + from_right(y[2 * n :])


def pairs(weights, windows):
    out = []
    for i in range(0, len(windows), 2):
        y = dot(weights, jnp.concatenate(windows[i : i + 2], axis=1))
        out += [y[:, :W], y[:, W:]]
    return out


def conv_mid(ref, weights, z, count):
    ys = pairs(weights, [triple(ref, z, h * C, 3 * C) for h in range(count)])
    return jnp.concatenate([join(y) for y in ys], axis=0)


def conv_mid_back(ref, weights, z, count):
    windows = [
        jnp.concatenate(
            [
                ref[z + 2 - oz, (row + 2 - oy) * C : (row + 3 - oy) * C, :]
                for oz in range(3)
                for oy in range(3)
            ],
            axis=0,
        )
        for row in range(count)
    ]
    ys = pairs(weights, windows)
    return jnp.concatenate(
        [y[C : 2 * C] + from_right(y[0:C]) + from_left(y[2 * C :]) for y in ys], axis=0
    )


def conv_last(ref, weights, slices):
    ys = pairs(weights, [triple(ref, z, 0, 6 * C) for z in range(slices)])
    return [join(y) for y in ys]


def banded_tail(tail):
    moved = []
    for h in range(H):
        parts = []
        for oz in range(3):
            if h:
                parts.append(jnp.zeros((16, C * h), F32))
            parts.append(tail[:, 96 * oz : 96 * oz + 96])
            if h < 3:
                parts.append(jnp.zeros((16, 96 - C * h), F32))
        moved.append(jnp.concatenate(parts, axis=1))
    rows = []
    for ox in range(3):
        rows += [m[ox : ox + 1] for m in moved] + [jnp.zeros((8 - H, 18 * C), F32)]
    return jnp.concatenate(rows, axis=0).astype(BF16)


def project(field, high, low):
    parts = []
    at = lax.broadcasted_iota(jnp.int32, (HI, W), 0).astype(F32)
    for h in range(H):
        match = high[h : h + 1, :] == at
        rows = [jnp.where(match, field[h][r : r + 1, :], 0.0) for r in range(field[h].shape[0])]
        parts.append(jnp.concatenate(rows, axis=0))
    part = jnp.concatenate(parts, axis=1)
    head = part.astype(BF16)
    rest = (part - head.astype(F32)).astype(BF16)
    n = part.shape[0]
    both = dot_nt(jnp.concatenate([head, rest], axis=0), low)
    return both[:n] + both[n:]


def local_kernel(cot, bins, first, second, third, pack_out, lows_out, first_out, wide_out, last_out,
                 first_back, wide_back, last_back):
    head = cot[...].astype(BF16)
    pack_out[0:4] = head
    pack_out[4:8] = (cot[...] - head.astype(F32)).astype(BF16)
    pack_out[8:16] = (bins[...] >> 7).astype(F32).astype(BF16)
    pack_out[16:24] = (bins[...] & 127).astype(F32).astype(BF16)
    for a in range(ANG):
        for h in range(H):
            lows_out[a, :, h * W : (h + 1) * W] = low_match(bins[a, h : h + 1, :] & 127)
    first_out[...] = banded(base_of(first[...], False), 10, 0)
    first_back[...] = banded(base_of(third[...], True), 8, 1)
    last_out[...] = tail_of(third[...], False)
    last_back[...] = tail_of(first[...], True)
    for ox in range(3):
        blocks = [second[q * 3 + ox] for q in range(9)]
        wide_out[ox * C : (ox + 1) * C, :] = jnp.concatenate(blocks, axis=1)
        blocks = jnp.concatenate(blocks, axis=0).astype(F32)
        wide_back[ox * C : (ox + 1) * C, :] = blocks.T.astype(BF16)


def near_slot(pos, count, slots, step):
    at = pos[0] + step
    rows = slots[jnp.clip(at, 0, count - 1)].astype(F32)
    return jnp.where((at >= 0) & (at < count), rows, 0.0)


def in_order(at, first, second):
    even = (at & 1) == 0
    return jnp.where(even, second, first), jnp.where(even, first, second)


def pack_kernel(pos, first, second, own, local, out):
    before, after = in_order(pos[0], first[...].astype(F32), second[...].astype(F32))
    out[0:4] = before.astype(BF16)
    out[4:8] = own[...]
    out[8:12] = after.astype(BF16)
    out[12:36] = local[...]


def forward_kernel(depth_count, plane_count, pos, swap_a, swap_b, mid, lows, first, second, third,
                   vc_out, act1_out, slope1_out, act2_out, slope2_out, rays_out,
                   vs, v3, vcs, a1, a2):
    depth_at = pos[0] * Z
    plane_at = pos[1] * H
    nz, nh = depth_count * Z, plane_count * H
    vs[...] = jnp.zeros_like(vs)
    lo, hi = in_order(pos[1], swap_a[0:12].astype(F32), swap_b[0:12].astype(F32))
    vs[:, 0:4, :] = lo
    vs[:, 4:8, :] = mid[0:12].astype(F32)
    vs[:, 8:12, :] = hi
    three_shifts(v3, vs[...].reshape(12 * 16, W), 12)
    vcs[...] = jnp.zeros_like(vcs)
    for z in range(8):
        for h in range(H):
            for oz in range(3):
                vcs[z * H + h, oz * 3 : oz * 3 + 3, :] = vs[z + 1 + oz, h + 3 : h + 6, :]
    vc_out[...] = vcs[...].astype(BF16)
    weights = first[...]
    ok_rows = row_ok(10 * C, plane_at - 3, nh)
    ps = pairs(weights, [v3[z + 1 : z + 4].reshape(144, W) for z in range(8)])
    for z in range(8):
        p = ps[z]
        sigma = jax.nn.sigmoid(p)
        at = depth_at + (z - 2)
        ok = ok_rows & (at >= 0) & (at < nz)
        act = jnp.where(ok, p * sigma, 0.0).astype(BF16)
        a1[z] = act
        act1_out[z] = act[2 * C : 8 * C]
        slope1_out[z] = (sigma * (1.0 + p * (1.0 - sigma)))[2 * C : 8 * C]
    wide = second[...]
    ok_rows = row_ok(8 * C, plane_at - 2, nh)
    for z in range(6):
        p = conv_mid(a1, wide, z, 8)
        sigma = jax.nn.sigmoid(p)
        at = depth_at + (z - 1)
        ok = ok_rows & (at >= 0) & (at < nz)
        act = jnp.where(ok, p * sigma, 0.0).astype(BF16)
        slope2_out[z] = sigma * (1.0 + p * (1.0 - sigma))
        a2[z] = act[C : 7 * C]
        act2_out[z] = act[C : 7 * C]
    last = third[...]
    local = mid[12:36].astype(F32)
    cot = local[0:4] + local[4:8]
    field = []
    dens = [vs[z + 4, 4:8, :] - y[0:H] for z, y in enumerate(conv_last(a2, last, Z))]
    for h in range(H):
        rows = [den[h : h + 1] for den in dens]
        for z in range(Z):
            rows.append(cot[z, h : h + 1, :])
        field.append(jnp.concatenate(rows, axis=0))
    for a in range(ANG):
        tile = project(field, local[8 + a], lows[a]).reshape(2, Z, HI, 128)
        head = tile[0].astype(BF16).astype(F32)
        rows = jnp.concatenate([head, tile[0] - head, tile[1]], axis=1)
        rays_out[a * Z : (a + 1) * Z] = rows.astype(BF16)


def weigh_kernel(planes, rays, chosen, out):
    each = TILES // planes
    total = jnp.sum(rays[...].astype(F32), axis=0)
    for t in range(each):
        at = t * 3 * HI
        forward = total[at : at + HI] + total[at + HI : at + 2 * HI]
        turned = total[at + 2 * HI : at + 3 * HI]
        ratio = (forward - chosen[t]) / delta_scale
        inner = 1.0 + ratio * ratio
        weighted = turned / (inner * jnp.sqrt(inner))
        weighted = jnp.broadcast_to(weighted[None], (planes, HI, 128))
        out[:, t * HI : (t + 1) * HI, :] = weighted.astype(BF16)


def back_kernel(plane_count, pos, rays, swap_a, swap_b, mid, cot, slab_out, own_out, slab):
    plane_at = pos[1] * H
    nh = plane_count * H
    lo, hi = in_order(pos[1], swap_a[12:36].astype(F32), swap_b[12:36].astype(F32))
    packs = [lo, mid[12:36].astype(F32), hi]
    at = lax.broadcasted_iota(jnp.int32, (HI, W), 0).astype(F32)
    spans = range(1, 11)
    total = [None] * len(spans)
    for a in range(ANG):
        rows = rays[a * Z : (a + 1) * Z].astype(F32).reshape(Z * HI, 128).astype(BF16)
        highs = [packs[h // H][8 + a, h % H : h % H + 1, :] for h in spans]
        lows = [packs[h // H][16 + a, h % H : h % H + 1, :] for h in spans]
        low = jnp.concatenate([low_match(b) for b in lows], axis=1)
        spread = dot(rows, low)
        for i, b in enumerate(highs):
            match = jnp.concatenate([b == at] * Z, axis=0)
            term = jnp.where(match, spread[:, i * W : (i + 1) * W], 0.0)
            total[i] = term if total[i] is None else total[i] + term
    slab[...] = jnp.zeros_like(slab)
    for i, h in enumerate(spans):
        summed = jnp.sum(total[i].reshape(Z, HI, W), axis=1)
        if H <= h < 2 * H:
            rows = cot[:, h - H, :]
        else:
            pack = packs[h // H]
            rows = pack[0:4, h % H, :] + pack[4:8, h % H, :]
        field = rows - (0.25 / ANG) * summed
        row = plane_at + h - H
        slab[h] = jnp.where((row >= 0) & (row < nh), -field, 0.0)
        if H <= h < 2 * H:
            own_out[h - H] = field
    slab_out[...] = slab[...].astype(BF16)


def backward_kernel(depth_count, plane_count, pos, slab, own, first, second, third,
                    vc, act1, slope1, act2, slope2,
                    volume_out, terms_out,
                    gs, v3, gx, gm, gm3, low, low3, terms, side):
    depth_at = pos[0] * Z
    plane_at = pos[1] * H
    nz, nh = depth_count * Z, plane_count * H
    gs[...] = jnp.zeros_like(gs)
    for h in range(12):
        gs[2:6, h, :] = slab[h].astype(F32)
    three_shifts(v3, gs[...].reshape(128, W), 8)
    gx[...] = jnp.zeros_like(gx)
    rows = gs[2:6, 4:8, :].reshape(16, W)
    gx[:, 0, :] = from_right(rows)
    gx[:, 1, :] = rows
    gx[:, 2, :] = from_left(rows)
    edge = jnp.zeros((2, 8 * C, W), BF16)
    gm[0:2] = edge
    gm[8:10] = edge
    edge = jnp.zeros((2, 6 * C, W), BF16)
    low[0:2] = edge
    low[10:12] = edge
    weights = third[...]
    ok_rows = row_ok(8 * C, plane_at - 2, nh)
    ys = pairs(weights, [v3[z : z + 3].reshape(144, W) for z in range(6)])
    for z in range(6):
        y = ys[z]
        at = depth_at + (z - 1)
        ok = ok_rows & (at >= 0) & (at < nz)
        g = jnp.where(ok, y * slope2[z], 0.0).astype(BF16)
        gm[z + 2] = g
        inner = g[2 * C : 6 * C].astype(F32)
        gm3[z, 0] = from_right(inner).astype(BF16)
        gm3[z, 1] = g[2 * C : 6 * C]
        gm3[z, 2] = from_left(inner).astype(BF16)

    def shifted(ref, slices):
        return jnp.concatenate(
            [
                jnp.concatenate([ref[z, ox, h * C : (h + 1) * C, :] for ox in range(3)], axis=0)
                for z in range(slices)
                for h in range(H)
            ],
            axis=1,
        )

    def windows(ref, slices):
        rows = jnp.concatenate(
            [triple(ref, z, h * C, 3 * C) for z in range(slices) for h in range(H)], axis=1
        )
        return jnp.concatenate([rows, jnp.zeros((96, slices * H * W), BF16)], axis=0)

    terms[...] = jnp.zeros_like(terms)
    term = dot_nt(shifted(gm3, 6), windows(act1, 6))
    terms[0:96] = term[:, 0:128]
    terms[96:192] = term[:, 128:256]
    tail = term[0:24, 256:384]
    for i in range(1, 4):
        tail = tail + pltpu.roll(term[24 * i : 24 * i + 24, 256:384], 32 * i, 1)
    terms[192:216] = tail
    gx_all = jnp.concatenate([gx[i] for i in range(16)], axis=1).astype(BF16)
    term = dot_nt(gx_all, windows(act2, 4))
    for i in range(3):
        terms[216 + 3 * i : 219 + 3 * i] = term[0:3, 128 * i : 128 * i + 128]
    wide = second[...]
    ok_rows = row_ok(6 * C, plane_at - 1, nh)
    for z in range(8):
        y = conv_mid_back(gm, wide, z, 6)
        at = depth_at + (z - 2)
        ok = ok_rows & (at >= 0) & (at < nz)
        g = jnp.where(ok, y * slope1[z], 0.0).astype(BF16)
        low[z + 2] = g
        inner = g[C : 5 * C].astype(F32)
        low3[z, 0] = from_right(inner).astype(BF16)
        low3[z, 1] = g[C : 5 * C]
        low3[z, 2] = from_left(inner).astype(BF16)
    vc_all = jnp.concatenate([vc[i] for i in range(32)], axis=1)
    rows = jnp.concatenate([shifted(low3, 8), jnp.zeros((32, 32 * W), BF16)], axis=0)
    terms[225:234] = dot_nt(vc_all, rows)[0:9]
    chunk = 256 // depth_count
    terms_out[:, 0:chunk, :] = terms[...].reshape(depth_count, chunk, 128).astype(BF16)
    terms_out[:, chunk : chunk + 16, :] = jnp.zeros((depth_count, 16, 128), BF16)
    side[...] = jnp.zeros_like(side)
    last = first[...]
    for z, y in enumerate(conv_last(low, last, 10)):
        if 3 <= z < 7:
            volume_out[z - 3] = own[:, z - 3, :] + y[0:H]
        else:
            at = (z % 7) * H
            side[z // 7, at : at + H, :] = y[0:H]

    @pl.when(pos[0] > 0)
    def _():
        terms_out[pos[0] - 1, chunk : chunk + 16, :] = side[0].astype(BF16)

    @pl.when(pos[0] < depth_count - 1)
    def _():
        terms_out[pos[0] + 1, chunk : chunk + 16, :] = side[1].astype(BF16)


def volume_kernel(count, pos, slots, volume, volume_out):
    before = near_slot(pos, count, slots, -1)[256 // count :]
    after = near_slot(pos, count, slots, 1)[256 // count :]
    for z in range(Z):
        rows = volume[z]
        if z < 3:
            rows = rows + before[z * H : (z + 1) * H]
        if z > 0:
            rows = rows + after[(z - 1) * H : z * H]
        volume_out[z] = rows


def unpack_kernel(scale, sums, in_out, mid_out, out_out):
    full = sums[...].astype(F32).reshape(256, 128) * scale
    quarters = [full] + [pltpu.roll(full, 128 - 32 * j, 1) for j in range(1, 4)]
    last = jnp.concatenate([q[192:216, 0:C] for q in quarters], axis=0)
    for q in range(9):
        for ox in range(3):
            if q < 8:
                start = 96 * (q // 4) + C * ox
                mid_out[q * 3 + ox] = quarters[q % 4][start : start + C, 0:C]
            else:
                mid_out[q * 3 + ox] = last[C * ox : C * ox + C]
        start = 216 + 3 * (q // 4)
        out_out[q * 3 : q * 3 + 3, :] = quarters[q % 4][start : start + 3, 0:C]
        for ox in range(3):
            in_out[q * 3 + ox : q * 3 + ox + 1, :] = quarters[ox][225 + q : 226 + q, 0:C]


def call(kernel, out_shapes, scratch, *args):
    specs = [pl.BlockSpec(memory_space=pltpu.VMEM) for _ in args]
    if args[0].dtype == jnp.int32 and args[0].ndim == 1:
        specs[0] = pl.BlockSpec(memory_space=pltpu.SMEM)
    return pl.pallas_call(
        kernel,
        out_shape=[jax.ShapeDtypeStruct(s, d) for s, d in out_shapes],
        in_specs=specs,
        out_specs=[pl.BlockSpec(memory_space=pltpu.VMEM) for _ in out_shapes],
        scratch_shapes=[pltpu.VMEM(s, d) for s, d in scratch],
        compiler_params=pltpu.CompilerParams(vmem_limit_bytes=40 * 1024 * 1024),
    )(*args)


def swaps(cells, axis):
    count = lax.axis_size(axis)
    first = [(i, i ^ 1) for i in range(count)]
    second = [(i, i + 1 if i % 2 else i - 1) for i in range(1, count - 1)]
    return lax.ppermute(cells, axis, first), lax.ppermute(cells, axis, second)


def scatter_to(cells, axis):
    return lax.all_to_all(cells, axis, 0, 0, tiled=True)


def per_device(volume, cotangent, kernel_in, kernel_mid, kernel_out, measured, angle_ids, ray_bins):
    depths, planes = lax.axis_size(DEPTH), lax.axis_size(PLANE)
    depth_at, plane_at = lax.axis_index(DEPTH), lax.axis_index(PLANE)
    pos = jnp.stack([depth_at, plane_at]).astype(jnp.int32)

    v_first, v_second = swaps(volume, DEPTH)
    local, lows, first, wide, last, first_back, wide_back, last_back = call(
        local_kernel,
        [
            ((24, H, W), BF16),
            ((ANG, 128, H * W), BF16),
            ((10 * C, 144), BF16),
            ((3 * C, 9 * C), BF16),
            ((24, 18 * C), BF16),
            ((8 * C, 144), BF16),
            ((3 * C, 9 * C), BF16),
            ((24, 18 * C), BF16),
        ],
        [],
        cotangent, ray_bins, kernel_in, kernel_mid, kernel_out,
    )
    pack = call(pack_kernel, [((36, H, W), BF16)], [], pos, v_first, v_second, volume, local)[0]
    p_first, p_second = swaps(pack, PLANE)

    vc, act1, slope1, act2, slope2, rays = call(
        functools.partial(forward_kernel, depths, planes),
        [
            ((32, 16, W), BF16),
            ((8, 6 * C, W), BF16),
            ((8, 6 * C, W), F32),
            ((6, 6 * C, W), BF16),
            ((6, 8 * C, W), F32),
            ((TILES, 3 * HI, 128), BF16),
        ],
        [
            ((12, 16, W), F32),
            ((12, 48, W), BF16),
            ((32, 16, W), F32),
            ((8, 10 * C, W), BF16),
            ((6, 6 * C, W), BF16),
        ],
        pos, p_first, p_second, pack, lows, first, wide, last,
    )
    each = TILES // planes
    gathered = scatter_to(rays.reshape(planes, each * 3 * HI, 128), PLANE)
    tiles = plane_at * each + jnp.arange(each)
    chosen = jnp.stack(
        [
            lax.dynamic_slice(measured, (tiles[t] % Z, angle_ids[tiles[t] // Z], 0), (1, 1, BINS))
            for t in range(each)
        ]
    ).reshape(each, HI, 128)
    spread = call(
        functools.partial(weigh_kernel, planes),
        [((planes, each * HI, 128), BF16)],
        [],
        gathered, chosen,
    )[0]
    weighted = scatter_to(spread, PLANE).reshape(TILES, HI, 128)
    slab, own = call(
        functools.partial(back_kernel, planes),
        [((12, Z, W), BF16), ((H, Z, W), F32)],
        [((12, Z, W), F32)],
        pos, weighted, p_first, p_second, pack, cotangent,
    )
    partial, terms = call(
        functools.partial(backward_kernel, depths, planes),
        [((Z, H, W), F32), ((depths, 256 // depths + 16, 128), BF16)],
        [
            ((8, 16, W), F32),
            ((8, 48, W), BF16),
            ((16, 16, W), F32),
            ((10, 8 * C, W), BF16),
            ((6, 3, 4 * C, W), BF16),
            ((12, 6 * C, W), BF16),
            ((8, 3, 4 * C, W), BF16),
            ((256, 128), F32),
            ((2, 16, W), F32),
        ],
        pos, slab, own, last_back, wide_back, first_back, vc, act1, slope1, act2, slope2,
    )
    chunk = 256 // depths

    def spread_sum(cells, count):
        total = jnp.sum(cells[:, :chunk].astype(F32), axis=0, keepdims=True).astype(BF16)
        return jnp.broadcast_to(total, (count,) + total.shape[1:])

    slots = scatter_to(terms, DEPTH)
    sums = scatter_to(spread_sum(slots, planes), PLANE)
    sums = scatter_to(spread_sum(sums, depths), DEPTH)
    cell_count = Z * depths * H * planes * W
    grad_volume = call(
        functools.partial(volume_kernel, depths), [((Z, H, W), F32)], [], pos, slots, partial
    )[0]
    got_in, got_mid, got_out = call(
        functools.partial(unpack_kernel, float(cell_count) ** (-0.5)),
        [((27, C), F32), ((27, C, C), F32), ((27, C), F32)],
        [],
        sums,
    )
    return (grad_volume, got_in, got_mid, got_out)


def solution(mesh):
    placed = (
        P(DEPTH, PLANE, None),
        P(DEPTH, PLANE, None),
        P(),
        P(),
        P(),
        P(DEPTH, None, None),
        P(),
        P(None, PLANE, None),
    )
    return jax.shard_map(
        per_device,
        mesh=mesh,
        in_specs=placed,
        out_specs=(P(DEPTH, PLANE, None), P(), P(), P()),
        check_vma=False,
    )
```

```python
import functools

import jax
import jax.numpy as jnp
from jax import lax
from jax.experimental import pallas as pl
from jax.experimental.pallas import tpu as pltpu
from jax.sharding import PartitionSpec as P

BINS = 1024
ANG = 8
C = 32
W = 128
Z = 4
H = 4
HI = BINS // 128
TILES = ANG * Z

delta_scale = 6.0

DEPTH = "depth"
PLANE = "plane"
F32 = jnp.float32
BF16 = jnp.bfloat16


def lanes_of(shape):
    return lax.broadcasted_iota(jnp.int32, shape, len(shape) - 1)


def from_left(x):
    lane = lanes_of(x.shape)
    return jnp.where(lane > 0, pltpu.roll(x, 1, x.ndim - 1), 0.0)


def from_right(x):
    lane = lanes_of(x.shape)
    return jnp.where(lane < W - 1, pltpu.roll(x, W - 1, x.ndim - 1), 0.0)


def dot(a, b):
    return jnp.dot(a, b, preferred_element_type=F32)


def dot_nt(a, b):
    return lax.dot_general(a, b, (((1,), (1,)), ((), ())), preferred_element_type=F32)


def row_ok(rows, first, count):
    at = lax.broadcasted_iota(jnp.int32, (rows, W), 0) // C + first
    return (at >= 0) & (at < count)


def banded(base, height, shift):
    rows = [pltpu.roll(base, h + shift, 1) if h + shift else base for h in range(height)]
    return jnp.concatenate(rows, axis=0)[:, :144].astype(BF16)


def base_of(kernel, flip):
    lane = lanes_of((27, 256))
    oz, ox, oy = lane // 48, (lane % 48) // 16, lane % 16
    at = oz * 9 + oy * 3 + ox
    row = lax.broadcasted_iota(jnp.int32, (27, 256), 0)
    take = ((26 - at if flip else at) == row) & (oy < 3) & (lane < 144)
    take = jnp.where(take, 1.0, 0.0).astype(BF16)
    return lax.dot_general(kernel, take, (((0,), (0,)), ((), ())), preferred_element_type=F32)


def tail_of(kernel, flip):
    spot = lax.broadcasted_iota(jnp.int32, (C, 9 * C), 0)
    spread = jnp.where(lanes_of((C, 9 * C)) % C == spot, 1.0, 0.0).astype(BF16)
    wide = dot(kernel, spread)
    row = lax.broadcasted_iota(jnp.int32, (27, 9 * C), 0)
    row = 26 - row if flip else row
    wide = jnp.where(row // 3 == lanes_of((27, 9 * C)) // C, wide, 0.0).astype(BF16)
    lane = lanes_of((16, 27))
    lane = 26 - lane if flip else lane
    pick = lane % 3 == lax.broadcasted_iota(jnp.int32, (16, 27), 0)
    return banded_tail(dot(jnp.where(pick, 1.0, 0.0).astype(BF16), wide))


def triple(ref, z, start, size):
    return jnp.concatenate([ref[z + oz, start : start + size, :] for oz in range(3)], axis=0)


def three_shifts(ref, flat, count):
    shape = (count, 16, W)
    ref[:, 0:16, :] = from_left(flat).reshape(shape).astype(BF16)
    ref[:, 16:32, :] = flat.reshape(shape).astype(BF16)
    ref[:, 32:48, :] = from_right(flat).reshape(shape).astype(BF16)


def low_match(low_row):
    n = low_row.shape[1]
    at = lax.broadcasted_iota(jnp.int32, (128, n), 0).astype(low_row.dtype)
    return jnp.where(low_row == at, 1.0, 0.0).astype(BF16)


def join(y):
    n = y.shape[0] // 3
    return y[n : 2 * n] + from_left(y[0:n]) + from_right(y[2 * n :])


def pairs(weights, windows):
    out = []
    for i in range(0, len(windows), 2):
        y = dot(weights, jnp.concatenate(windows[i : i + 2], axis=1))
        out += [y[:, :W], y[:, W:]]
    return out


def conv_mid(ref, weights, z, count):
    ys = pairs(weights, [triple(ref, z, h * C, 3 * C) for h in range(count)])
    return jnp.concatenate([join(y) for y in ys], axis=0)


def conv_mid_back(ref, weights, z, count):
    windows = [
        jnp.concatenate(
            [
                ref[z + 2 - oz, (row + 2 - oy) * C : (row + 3 - oy) * C, :]
                for oz in range(3)
                for oy in range(3)
            ],
            axis=0,
        )
        for row in range(count)
    ]
    ys = pairs(weights, windows)
    return jnp.concatenate(
        [y[C : 2 * C] + from_right(y[0:C]) + from_left(y[2 * C :]) for y in ys], axis=0
    )


def conv_last(ref, weights, slices):
    ys = pairs(weights, [triple(ref, z, 0, 6 * C) for z in range(slices)])
    return [join(y) for y in ys]


def banded_tail(tail):
    moved = []
    for h in range(H):
        parts = []
        for oz in range(3):
            if h:
                parts.append(jnp.zeros((16, C * h), F32))
            parts.append(tail[:, 96 * oz : 96 * oz + 96])
            if h < 3:
                parts.append(jnp.zeros((16, 96 - C * h), F32))
        moved.append(jnp.concatenate(parts, axis=1))
    rows = []
    for ox in range(3):
        rows += [m[ox : ox + 1] for m in moved] + [jnp.zeros((8 - H, 18 * C), F32)]
    return jnp.concatenate(rows, axis=0).astype(BF16)


def project(field, high, low):
    parts = []
    at = lax.broadcasted_iota(jnp.int32, (HI, W), 0).astype(F32)
    for h in range(H):
        match = high[h : h + 1, :] == at
        rows = [jnp.where(match, field[h][r : r + 1, :], 0.0) for r in range(field[h].shape[0])]
        parts.append(jnp.concatenate(rows, axis=0))
    part = jnp.concatenate(parts, axis=1)
    head = part.astype(BF16)
    rest = (part - head.astype(F32)).astype(BF16)
    n = part.shape[0]
    both = dot_nt(jnp.concatenate([head, rest], axis=0), low)
    return both[:n] + both[n:]


def local_kernel(cot, bins, first, second, third, pack_out, lows_out, first_out, wide_out, last_out,
                 first_back, wide_back, last_back):
    head = cot[...].astype(BF16)
    pack_out[0:4] = head
    pack_out[4:8] = (cot[...] - head.astype(F32)).astype(BF16)
    pack_out[8:16] = (bins[...] >> 7).astype(F32).astype(BF16)
    pack_out[16:24] = (bins[...] & 127).astype(F32).astype(BF16)
    for a in range(ANG):
        for h in range(H):
            lows_out[a, :, h * W : (h + 1) * W] = low_match(bins[a, h : h + 1, :] & 127)
    first_out[...] = banded(base_of(first[...], False), 10, 0)
    first_back[...] = banded(base_of(third[...], True), 8, 1)
    last_out[...] = tail_of(third[...], False)
    last_back[...] = tail_of(first[...], True)
    for ox in range(3):
        blocks = [second[q * 3 + ox] for q in range(9)]
        wide_out[ox * C : (ox + 1) * C, :] = jnp.concatenate(blocks, axis=1)
        blocks = jnp.concatenate(blocks, axis=0).astype(F32)
        wide_back[ox * C : (ox + 1) * C, :] = blocks.T.astype(BF16)


def near_slot(pos, count, slots, step):
    at = pos[0] + step
    rows = slots[jnp.clip(at, 0, count - 1)].astype(F32)
    return jnp.where((at >= 0) & (at < count), rows, 0.0)


def in_order(at, first, second):
    even = (at & 1) == 0
    return jnp.where(even, second, first), jnp.where(even, first, second)


def pack_kernel(pos, first, second, own, local, out):
    before, after = in_order(pos[0], first[...].astype(F32), second[...].astype(F32))
    out[0:4] = before.astype(BF16)
    out[4:8] = own[...]
    out[8:12] = after.astype(BF16)
    out[12:36] = local[...]


def forward_kernel(depth_count, plane_count, pos, swap_b, swap_a, mid, lows, first, second, third,
                   vc_out, act1_out, slope1_out, act2_out, slope2_out, rays_out,
                   vs, v3, vcs, a1, a2):
    depth_at = pos[0] * Z
    plane_at = pos[1] * H
    nz, nh = depth_count * Z, plane_count * H
    vs[...] = jnp.zeros_like(vs)
    lo, hi = in_order(pos[1], swap_a[0:12].astype(F32), swap_b[0:12].astype(F32))
    vs[:, 0:4, :] = lo
    vs[:, 4:8, :] = mid[0:12].astype(F32)
    vs[:, 8:12, :] = hi
    three_shifts(v3, vs[...].reshape(12 * 16, W), 12)
    vcs[...] = jnp.zeros_like(vcs)
    for z in range(8):
        for h in range(H):
            for oz in range(3):
                vcs[z * H + h, oz * 3 : oz * 3 + 3, :] = vs[z + 1 + oz, h + 3 : h + 6, :]
    vc_out[...] = vcs[...].astype(BF16)
    weights = first[...]
    ok_rows = row_ok(10 * C, plane_at - 3, nh)
    ps = pairs(weights, [v3[z + 1 : z + 4].reshape(144, W) for z in range(8)])
    for z in range(8):
        p = ps[z]
        sigma = jax.nn.sigmoid(p)
        at = depth_at + (z - 2)
        ok = ok_rows & (at >= 0) & (at < nz)
        act = jnp.where(ok, p * sigma, 0.0).astype(BF16)
        a1[z] = act
        act1_out[z] = act[2 * C : 8 * C]
        slope1_out[z] = (sigma * (1.0 + p * (1.0 - sigma)))[2 * C : 8 * C]
    wide = second[...]
    ok_rows = row_ok(8 * C, plane_at - 2, nh)
    for z in range(6):
        p = conv_mid(a1, wide, z, 8)
        sigma = jax.nn.sigmoid(p)
        at = depth_at + (z - 1)
        ok = ok_rows & (at >= 0) & (at < nz)
        act = jnp.where(ok, p * sigma, 0.0).astype(BF16)
        slope2_out[z] = sigma * (1.0 + p * (1.0 - sigma))
        a2[z] = act[C : 7 * C]
        act2_out[z] = act[C : 7 * C]
    last = third[...]
    local = mid[12:36].astype(F32)
    cot = local[0:4] + local[4:8]
    field = []
    dens = [vs[z + 4, 4:8, :] - y[0:H] for z, y in enumerate(conv_last(a2, last, Z))]
    for h in range(H):
        rows = [den[h : h + 1] for den in dens]
        for z in range(Z):
            rows.append(cot[z, h : h + 1, :])
        field.append(jnp.concatenate(rows, axis=0))
    for a in range(ANG):
        tile = project(field, local[8 + a], lows[a]).reshape(2, Z, HI, 128)
        head = tile[0].astype(BF16).astype(F32)
        rows = jnp.concatenate([head, tile[0] - head, tile[1]], axis=1)
        rays_out[a * Z : (a + 1) * Z] = rows.astype(BF16)


def weigh_kernel(planes, rays, chosen, out):
    each = TILES // planes
    total = jnp.sum(rays[...].astype(F32), axis=0)
    for t in range(each):
        at = t * 3 * HI
        forward = total[at : at + HI] + total[at + HI : at + 2 * HI]
        turned = total[at + 2 * HI : at + 3 * HI]
        ratio = (forward - chosen[t]) / delta_scale
        inner = 1.0 + ratio * ratio
        weighted = turned / (inner * jnp.sqrt(inner))
        weighted = jnp.broadcast_to(weighted[None], (planes, HI, 128))
        out[:, t * HI : (t + 1) * HI, :] = weighted.astype(BF16)


def back_kernel(plane_count, pos, rays, swap_b, swap_a, mid, cot, slab_out, own_out, slab):
    plane_at = pos[1] * H
    nh = plane_count * H
    lo, hi = in_order(pos[1], swap_a[12:36].astype(F32), swap_b[12:36].astype(F32))
    packs = [lo, mid[12:36].astype(F32), hi]
    at = lax.broadcasted_iota(jnp.int32, (HI, W), 0).astype(F32)
    spans = range(1, 11)
    total = [None] * len(spans)
    for a in range(ANG):
        rows = rays[a * Z : (a + 1) * Z].astype(F32).reshape(Z * HI, 128).astype(BF16)
        highs = [packs[h // H][8 + a, h % H : h % H + 1, :] for h in spans]
        lows = [packs[h // H][16 + a, h % H : h % H + 1, :] for h in spans]
        spread = dot(rows, jnp.concatenate([low_match(b) for b in lows], axis=1))
        for i, b in enumerate(highs):
            match = jnp.concatenate([b == at] * Z, axis=0)
            term = jnp.where(match, spread[:, i * W : (i + 1) * W], 0.0)
            total[i] = term if total[i] is None else total[i] + term
    slab[...] = jnp.zeros_like(slab)
    for i, h in enumerate(spans):
        summed = jnp.sum(total[i].reshape(Z, HI, W), axis=1)
        if H <= h < 2 * H:
            rows = cot[:, h - H, :]
        else:
            pack = packs[h // H]
            rows = pack[0:4, h % H, :] + pack[4:8, h % H, :]
        field = rows - (0.25 / ANG) * summed
        row = plane_at + h - H
        slab[h] = jnp.where((row >= 0) & (row < nh), -field, 0.0)
        if H <= h < 2 * H:
            own_out[h - H] = field
    slab_out[...] = slab[...].astype(BF16)


def backward_kernel(depth_count, plane_count, pos, slab, own, first, second, third,
                    vc, act1, slope1, act2, slope2,
                    volume_out, terms_out,
                    gs, v3, gx, gm, gm3, low, low3, terms, side):
    depth_at = pos[0] * Z
    plane_at = pos[1] * H
    nz, nh = depth_count * Z, plane_count * H
    gs[...] = jnp.zeros_like(gs)
    for h in range(12):
        gs[2:6, h, :] = slab[h].astype(F32)
    three_shifts(v3, gs[...].reshape(128, W), 8)
    gx[...] = jnp.zeros_like(gx)
    rows = gs[2:6, 4:8, :].reshape(16, W)
    gx[:, 0, :] = from_right(rows)
    gx[:, 1, :] = rows
    gx[:, 2, :] = from_left(rows)
    edge = jnp.zeros((2, 8 * C, W), BF16)
    gm[0:2] = edge
    gm[8:10] = edge
    edge = jnp.zeros((2, 6 * C, W), BF16)
    low[0:2] = edge
    low[10:12] = edge
    weights = third[...]
    ok_rows = row_ok(8 * C, plane_at - 2, nh)
    ys = pairs(weights, [v3[z : z + 3].reshape(144, W) for z in range(6)])
    for z in range(6):
        y = ys[z]
        at = depth_at + (z - 1)
        ok = ok_rows & (at >= 0) & (at < nz)
        g = jnp.where(ok, y * slope2[z], 0.0).astype(BF16)
        gm[z + 2] = g
        inner = g[2 * C : 6 * C].astype(F32)
        gm3[z, 0] = from_right(inner).astype(BF16)
        gm3[z, 1] = g[2 * C : 6 * C]
        gm3[z, 2] = from_left(inner).astype(BF16)

    def shifted(ref, slices):
        return jnp.concatenate(
            [
                jnp.concatenate([ref[z, ox, h * C : (h + 1) * C, :] for ox in range(3)], axis=0)
                for z in range(slices)
                for h in range(H)
            ],
            axis=1,
        )

    def windows(ref, slices):
        rows = jnp.concatenate(
            [triple(ref, z, h * C, 3 * C) for z in range(slices) for h in range(H)], axis=1
        )
        return jnp.concatenate([rows, jnp.zeros((96, slices * H * W), BF16)], axis=0)

    terms[...] = jnp.zeros_like(terms)
    term = dot_nt(shifted(gm3, 6), windows(act1, 6))
    terms[0:96] = term[:, 0:128]
    terms[96:192] = term[:, 128:256]
    tail = term[0:24, 256:384]
    for i in range(1, 4):
        tail = tail + pltpu.roll(term[24 * i : 24 * i + 24, 256:384], 32 * i, 1)
    terms[192:216] = tail
    gx_all = jnp.concatenate([gx[i] for i in range(16)], axis=1).astype(BF16)
    term = dot_nt(gx_all, windows(act2, 4))
    for i in range(3):
        terms[216 + 3 * i : 219 + 3 * i] = term[0:3, 128 * i : 128 * i + 128]
    wide = second[...]
    ok_rows = row_ok(6 * C, plane_at - 1, nh)
    for z in range(8):
        y = conv_mid_back(gm, wide, z, 6)
        at = depth_at + (z - 2)
        ok = ok_rows & (at >= 0) & (at < nz)
        g = jnp.where(ok, y * slope1[z], 0.0).astype(BF16)
        low[z + 2] = g
        inner = g[C : 5 * C].astype(F32)
        low3[z, 0] = from_right(inner).astype(BF16)
        low3[z, 1] = g[C : 5 * C]
        low3[z, 2] = from_left(inner).astype(BF16)
    vc_all = jnp.concatenate([vc[i] for i in range(32)], axis=1)
    rows = jnp.concatenate([shifted(low3, 8), jnp.zeros((32, 32 * W), BF16)], axis=0)
    terms[225:234] = dot_nt(vc_all, rows)[0:9]
    chunk = 256 // depth_count
    terms_out[:, 0:chunk, :] = terms[...].reshape(depth_count, chunk, 128).astype(BF16)
    terms_out[:, chunk : chunk + 16, :] = jnp.zeros((depth_count, 16, 128), BF16)
    side[...] = jnp.zeros_like(side)
    last = first[...]
    for z, y in enumerate(conv_last(low, last, 10)):
        if 3 <= z < 7:
            volume_out[z - 3] = own[:, z - 3, :] + y[0:H]
        else:
            at = (z % 7) * H
            side[z // 7, at : at + H, :] = y[0:H]

    @pl.when(pos[0] > 0)
    def _():
        terms_out[pos[0] - 1, chunk : chunk + 16, :] = side[0].astype(BF16)

    @pl.when(pos[0] < depth_count - 1)
    def _():
        terms_out[pos[0] + 1, chunk : chunk + 16, :] = side[1].astype(BF16)


def unpack_kernel(scale, count, pos, sums, slots, volume, volume_out, in_out, mid_out, out_out):
    before = near_slot(pos, count, slots, -1)[256 // count :]
    after = near_slot(pos, count, slots, 1)[256 // count :]
    for z in range(Z):
        rows = volume[z]
        if z < 3:
            rows = rows + before[z * H : (z + 1) * H]
        if z > 0:
            rows = rows + after[(z - 1) * H : z * H]
        volume_out[z] = rows
    full = sums[...].astype(F32).reshape(256, 128) * scale
    quarters = [full] + [pltpu.roll(full, 128 - 32 * j, 1) for j in range(1, 4)]
    last = jnp.concatenate([q[192:216, 0:C] for q in quarters], axis=0)
    for q in range(9):
        for ox in range(3):
            if q < 8:
                start = 96 * (q // 4) + C * ox
                mid_out[q * 3 + ox] = quarters[q % 4][start : start + C, 0:C]
            else:
                mid_out[q * 3 + ox] = last[C * ox : C * ox + C]
        start = 216 + 3 * (q // 4)
        out_out[q * 3 : q * 3 + 3, :] = quarters[q % 4][start : start + 3, 0:C]
        for ox in range(3):
            in_out[q * 3 + ox : q * 3 + ox + 1, :] = quarters[ox][225 + q : 226 + q, 0:C]


def call(kernel, out_shapes, scratch, *args):
    specs = [pl.BlockSpec(memory_space=pltpu.VMEM) for _ in args]
    if args[0].dtype == jnp.int32 and args[0].ndim == 1:
        specs[0] = pl.BlockSpec(memory_space=pltpu.SMEM)
    return pl.pallas_call(
        kernel,
        out_shape=[jax.ShapeDtypeStruct(s, d) for s, d in out_shapes],
        in_specs=specs,
        out_specs=[pl.BlockSpec(memory_space=pltpu.VMEM) for _ in out_shapes],
        scratch_shapes=[pltpu.VMEM(s, d) for s, d in scratch],
        compiler_params=pltpu.CompilerParams(vmem_limit_bytes=40 * 1024 * 1024),
    )(*args)


def swaps(cells, axis):
    count = lax.axis_size(axis)
    first = [(i, i ^ 1) for i in range(count)]
    second = [(i, i + 1 if i % 2 else i - 1) for i in range(1, count - 1)]
    after = lax.ppermute(cells, axis, second)
    return lax.ppermute(cells, axis, first), after


def scatter_to(cells, axis):
    return lax.all_to_all(cells, axis, 0, 0, tiled=True)


def per_device(volume, cotangent, kernel_in, kernel_mid, kernel_out, measured, angle_ids, ray_bins):
    depths, planes = lax.axis_size(DEPTH), lax.axis_size(PLANE)
    depth_at, plane_at = lax.axis_index(DEPTH), lax.axis_index(PLANE)
    pos = jnp.stack([depth_at, plane_at]).astype(jnp.int32)

    v_first, v_second = swaps(volume, DEPTH)
    local, lows, first, wide, last, first_back, wide_back, last_back = call(
        local_kernel,
        [
            ((24, H, W), BF16),
            ((ANG, 128, H * W), BF16),
            ((10 * C, 144), BF16),
            ((3 * C, 9 * C), BF16),
            ((24, 18 * C), BF16),
            ((8 * C, 144), BF16),
            ((3 * C, 9 * C), BF16),
            ((24, 18 * C), BF16),
        ],
        [],
        cotangent, ray_bins, kernel_in, kernel_mid, kernel_out,
    )
    pack = call(pack_kernel, [((36, H, W), BF16)], [], pos, v_first, v_second, volume, local)[0]
    p_first, p_second = swaps(pack, PLANE)

    vc, act1, slope1, act2, slope2, rays = call(
        functools.partial(forward_kernel, depths, planes),
        [
            ((32, 16, W), BF16),
            ((8, 6 * C, W), BF16),
            ((8, 6 * C, W), F32),
            ((6, 6 * C, W), BF16),
            ((6, 8 * C, W), F32),
            ((TILES, 3 * HI, 128), BF16),
        ],
        [
            ((12, 16, W), F32),
            ((12, 48, W), BF16),
            ((32, 16, W), F32),
            ((8, 10 * C, W), BF16),
            ((6, 6 * C, W), BF16),
        ],
        pos, p_second, p_first, pack, lows, first, wide, last,
    )
    each = TILES // planes
    gathered = scatter_to(rays.reshape(planes, each * 3 * HI, 128), PLANE)
    tiles = plane_at * each + jnp.arange(each)
    chosen = jnp.stack(
        [
            lax.dynamic_slice(measured, (tiles[t] % Z, angle_ids[tiles[t] // Z], 0), (1, 1, BINS))
            for t in range(each)
        ]
    ).reshape(each, HI, 128)
    spread = call(
        functools.partial(weigh_kernel, planes),
        [((planes, each * HI, 128), BF16)],
        [],
        gathered, chosen,
    )[0]
    weighted = scatter_to(spread, PLANE).reshape(TILES, HI, 128)
    slab, own = call(
        functools.partial(back_kernel, planes),
        [((12, Z, W), BF16), ((H, Z, W), F32)],
        [((12, Z, W), F32)],
        pos, weighted, p_second, p_first, pack, cotangent,
    )
    partial, terms = call(
        functools.partial(backward_kernel, depths, planes),
        [((Z, H, W), F32), ((depths, 256 // depths + 16, 128), BF16)],
        [
            ((8, 16, W), F32),
            ((8, 48, W), BF16),
            ((16, 16, W), F32),
            ((10, 8 * C, W), BF16),
            ((6, 3, 4 * C, W), BF16),
            ((12, 6 * C, W), BF16),
            ((8, 3, 4 * C, W), BF16),
            ((256, 128), F32),
            ((2, 16, W), F32),
        ],
        pos, slab, own, last_back, wide_back, first_back, vc, act1, slope1, act2, slope2,
    )
    chunk = 256 // depths

    def spread_sum(cells, count):
        total = jnp.sum(cells[:, :chunk].astype(F32), axis=0, keepdims=True).astype(BF16)
        return jnp.broadcast_to(total, (count,) + total.shape[1:])

    slots = scatter_to(terms, DEPTH)
    sums = scatter_to(spread_sum(slots, planes), PLANE)
    sums = scatter_to(spread_sum(sums, depths), DEPTH)
    cell_count = Z * depths * H * planes * W
    grad_volume, got_in, got_mid, got_out = call(
        functools.partial(unpack_kernel, float(cell_count) ** (-0.5), depths),
        [((Z, H, W), F32), ((27, C), F32), ((27, C, C), F32), ((27, C), F32)],
        [],
        pos, sums, slots, partial,
    )
    return (grad_volume, got_in, got_mid, got_out)


def solution(mesh):
    placed = (
        P(DEPTH, PLANE, None),
        P(DEPTH, PLANE, None),
        P(),
        P(),
        P(),
        P(DEPTH, None, None),
        P(),
        P(None, PLANE, None),
    )
    return jax.shard_map(
        per_device,
        mesh=mesh,
        in_specs=placed,
        out_specs=(P(DEPTH, PLANE, None), P(), P(), P()),
        check_vma=False,
    )
```
